512 devices in a mesh: people: 32 (over z, core), blocks: 16 (over x, y).
Axes of the slice: x: 4, y: 4, z: 16, core: 2. Of those that a mesh axis runs over, the one named last changes fastest.
Arguments:
- allele_amounts: bfloat16 [131072, 8192], P('people', 'blocks'), may hold values from 0 to 2
- outcome_matrix: bfloat16 [131072, 16], P('people'), may hold values from -6 to 6
- shrinkage_factors: float32 [5], replicated, may hold values from 0.05 to 2
Outputs:
- ridge_coef: float32 [8192, 80], P('blocks')
- level1_gram: float32 [16, 80, 80], P('blocks')
- level1_cross: float32 [16, 80], P('blocks')
The draws below stay inside these ranges and needn't reach their ends.
All inputs are finite; a program needn't handle non-finite values.
Results may differ from the reference program's by a relative error of at most 0.002.
Values may be sent and summed in bfloat16 or wider, within the bound.
A program may use at most 64 MiB of HBM per device.

```python
import math
import jax
import jax.numpy as jnp
from jax import lax

VARS = 512
OUTCOME_TOTAL = 16
LAMBDA_GRID = 5
ITERS = 8
PEOPLE = 131072
BLOCKS = 16
VARIANTS = 8192


def draw_allele_amounts(key, part):
    key_freq, key_noise = jax.random.split(jax.random.fold_in(key, 11))
    frequency = jax.random.uniform(key_freq, (1, VARIANTS), jnp.float32, 0.05, 0.3)
    noise = jax.random.uniform(key_noise, (PEOPLE, VARIANTS), jnp.float32)
    row_frac = (jnp.arange(PEOPLE, dtype=jnp.float32) / PEOPLE)[:, None]
    strata = 0.5 + row_frac
    return (4.0 * frequency * strata * noise).astype(jnp.bfloat16)


def steps_of(rng, dims, cuts, smallest, high):
    loudness = 1.0
    for axis_at, shards_of in cuts:
        steps = jax.random.uniform(jax.random.fold_in(jax.random.fold_in(rng, 6), axis_at), (shards_of,), jnp.float32, smallest / len(cuts), high / len(cuts))
        loudness = loudness * jnp.repeat(jnp.exp(steps), dims[axis_at] // shards_of).reshape((-1,) + (1,) * (len(dims) - 1 - axis_at))
    return loudness


def bell_draw(own_key, dims, width, most, cuts=(), kind=jnp.bfloat16):
    result = width * jax.random.normal(own_key, dims, jnp.float32)
    if cuts:
        result = result * steps_of(own_key, dims, cuts, -0.22, 0.18)
    return jnp.clip(result, -most, most).astype(kind)


def setup_inputs(seed: int = 0) -> dict:
    seeds = jax.random.split(jax.random.key(seed), 4)
    return {
        "allele_amounts": draw_allele_amounts(jax.random.fold_in(seeds[3], 71), 0),
        "outcome_matrix": bell_draw(seeds[1], (PEOPLE, OUTCOME_TOTAL), 1.0, 6.0, ((0, 32),)),
        "shrinkage_factors": jnp.clip(jnp.exp(jax.random.uniform(seeds[2], (LAMBDA_GRID,), jnp.float32, math.log(0.05), math.log(2.0))), 0.05, 2.0),
    }


def polynomial_iterate(scaled_covariance, target_vector, shrinkage_factors, eigenvalue_ceiling):
    shrinkage_vector = jnp.tile(shrinkage_factors, OUTCOME_TOTAL)
    starting_response = jnp.repeat(target_vector, LAMBDA_GRID, axis=1)
    radius = eigenvalue_ceiling / 2.0
    middle = shrinkage_vector + radius
    center = middle / radius
    weight = 1.0 / center
    shrunk_estimate = jnp.zeros_like(starting_response)
    remain = starting_response
    heading = remain / middle
    for sweep in range(ITERS):
        shrunk_estimate = shrunk_estimate + heading
        if sweep < ITERS - 1:
            remain = remain - (jnp.dot(scaled_covariance, heading, precision=lax.Precision.HIGHEST) + shrinkage_vector * heading)
            weight_next = 1.0 / (2.0 * center - weight)
            heading = weight_next * weight * heading + 2.0 * weight_next / radius * remain
            weight = weight_next
    return shrunk_estimate

def reference(allele_amounts, outcome_matrix, shrinkage_factors):
    headcount = allele_amounts.shape[0]
    trait_sums = lax.optimization_barrier(jnp.sum(outcome_matrix, axis=0, dtype=jnp.float32))
    coef_parts = []
    prediction_parts = []
    for which_block in range(BLOCKS):
        block_dose = allele_amounts[:, which_block * VARS:(which_block + 1) * VARS]
        col_sums = lax.optimization_barrier(jnp.sum(block_dose, axis=0, dtype=jnp.float32))
        square_sums = lax.optimization_barrier(jnp.sum(jnp.square(block_dose.astype(jnp.float32)), axis=0))
        gram_raw = lax.dot_general(block_dose, block_dose, (((0,), (0,)), ((), ())), preferred_element_type=jnp.float32)
        cross_raw = lax.dot_general(block_dose, outcome_matrix, (((0,), (0,)), ((), ())), preferred_element_type=jnp.float32)
        average = col_sums / headcount
        spread = jnp.sqrt(square_sums / headcount - average * average + 1e-05)
        scaled_covariance = (gram_raw / headcount - jnp.outer(average, average)) / jnp.outer(spread, spread)
        target_vector = math.sqrt(headcount) * (cross_raw / headcount - jnp.outer(average, trait_sums / headcount)) / spread[:, None]
        eigenvalue_ceiling = jnp.max(lax.optimization_barrier(jnp.sum(jnp.abs(scaled_covariance), axis=1)))
        shrunk_estimate = polynomial_iterate(scaled_covariance, target_vector, shrinkage_factors, eigenvalue_ceiling)
        coef_parts.append(shrunk_estimate)
        scaled_coef = (shrunk_estimate / (spread[:, None] * math.sqrt(VARS))).astype(jnp.bfloat16)
        offset = jnp.dot(average, scaled_coef.astype(jnp.float32), precision=lax.Precision.HIGHEST)
        model_predicted_phenotypes = (jnp.dot(block_dose, scaled_coef, preferred_element_type=jnp.float32) - offset).astype(jnp.bfloat16)
        prediction_parts.append(model_predicted_phenotypes)
    ridge_coef = jnp.concatenate(coef_parts, axis=0)
    grams = []
    crosses = []
    for phenotype_position in range(OUTCOME_TOTAL):
        layered_blocks = jnp.concatenate([part[:, phenotype_position * LAMBDA_GRID:(phenotype_position + 1) * LAMBDA_GRID] for part in prediction_parts], axis=1)
        grams.append(jnp.dot(layered_blocks.T, layered_blocks, preferred_element_type=jnp.float32) / headcount)
        crosses.append(jnp.dot(layered_blocks.T, outcome_matrix[:, phenotype_position], preferred_element_type=jnp.float32) / math.sqrt(headcount))
    return (ridge_coef, jnp.stack(grams), jnp.stack(crosses))
```

```python
import functools
import math

import jax
import jax.numpy as jnp
from jax import lax
from jax.experimental import pallas as pl
from jax.experimental.pallas import tpu as pltpu
from jax.sharding import PartitionSpec as P

VARS = 512
TRAITS = 16
LAMBDAS = 5
ITERS = 8
SLOT = 8
PARTS = 16
MESH = pl.DeviceIdType.MESH
F32 = jnp.float32
BF16 = jnp.bfloat16
HIGHEST = lax.Precision.HIGHEST

TILE = 128
TILES = [(i, j) for i in range(VARS // TILE) for j in range(i, VARS // TILE)]
CROSS_AT = len(TILES) * TILE
SUMS_AT = CROSS_AT + TRAITS * (VARS // TILE)
TRAIT_AT = SUMS_AT + VARS // TILE
USED = SUMS_AT + 8
CONTRACT_ROWS = (((0,), (0,)), ((), ()))
CONTRACT_LANES = (((1,), (1,)), ((), ()))


def piece_rows(chips):
    return -(-USED // (2 * chips * 8)) * 8


def iota(shape, dim):
    return lax.broadcasted_iota(jnp.int32, shape, dim)


def far_first(n):
    return sorted(range(1, n), key=lambda d: -min(d, n - d))


def near_first(n):
    return sorted(range(1, n), key=lambda d: min(d, n - d))


def partial_kernel(x_ref, y_ref, out_ref, top, low, cross, sums, trait):
    step = pl.program_id(0)

    @pl.when(step == 0)
    def _():
        top[...] = jnp.zeros_like(top)
        low[...] = jnp.zeros_like(low)
        cross[...] = jnp.zeros_like(cross)
        sums[...] = jnp.zeros_like(sums)
        trait[...] = jnp.zeros_like(trait)

    half = VARS // 2
    x = x_ref[...]
    y = y_ref[...]
    top[...] += lax.dot_general(x[:, :half], x, CONTRACT_ROWS, preferred_element_type=F32)
    low[...] += lax.dot_general(
        x[:, half:], x[:, half:], CONTRACT_ROWS, preferred_element_type=F32
    )
    cross[...] += lax.dot_general(y, x, CONTRACT_ROWS, preferred_element_type=F32)
    sums[...] += jnp.dot(jnp.ones((8, x.shape[0]), BF16), x, preferred_element_type=F32)
    trait[...] += jnp.sum(y.astype(F32), axis=0, keepdims=True)

    @pl.when(step == pl.num_programs(0) - 1)
    def _():
        for at, (i, j) in enumerate(TILES):
            rows = slice(at * TILE, (at + 1) * TILE)
            if i * TILE < half:
                out_ref[rows, :] = top[i * TILE:(i + 1) * TILE, j * TILE:(j + 1) * TILE]
            else:
                a, b = i * TILE - half, j * TILE - half
                out_ref[rows, :] = low[a:a + TILE, b:b + TILE]
        for j in range(VARS // TILE):
            at = CROSS_AT + j * TRAITS
            out_ref[at:at + TRAITS, :] = cross[:, j * TILE:(j + 1) * TILE]
        out_ref[SUMS_AT:, :] = jnp.zeros((out_ref.shape[0] - SUMS_AT, TILE), F32)
        for j in range(VARS // TILE):
            out_ref[SUMS_AT + j:SUMS_AT + j + 1, :] = sums[0:1, j * TILE:(j + 1) * TILE]
        out_ref[TRAIT_AT:TRAIT_AT + 1, 0:TRAITS] = trait[...]


def position():
    person = lax.axis_index("people")
    return lax.div(person, 2), lax.rem(person, 2), lax.axis_index("blocks")


def remote(src, dst, send, recv, people, block):
    return pltpu.make_async_remote_copy(
        src_ref=src, dst_ref=dst, send_sem=send, recv_sem=recv,
        device_id=(people, block), device_id_type=MESH,
    )


def signal(people, block):
    pl.semaphore_signal(
        pltpu.get_barrier_semaphore(), inc=1, device_id=(people, block), device_id_type=MESH
    )


def people_sum_kernel(
    chips, in_ref, out_ref, half, mine, slots, full,
    pair_send, pair_recv, spread_send, spread_recv, gather_send, gather_recv, pass_send, pass_recv,
):
    z, c, b = position()
    other = 1 - c
    piece = slots.shape[1]
    rows = chips * piece
    signal(2 * z + other, b)
    for d in range(1, chips):
        signal(2 * lax.rem(z + d, chips) + c, b)
    pl.semaphore_wait(pltpu.get_barrier_semaphore(), chips)

    def own(core, chip):
        return pl.ds(pl.multiple_of(core * rows + chip * piece, 8), piece)

    pair = remote(
        in_ref.at[pl.ds(pl.multiple_of(other * rows, 8), rows)], half,
        pair_send, pair_recv, 2 * z + other, b,
    )
    pair.start()
    pair.wait()
    mine[...] = in_ref[pl.ds(pl.multiple_of(c * rows, 8), rows), :] + half[...]
    spread = {}
    for d in far_first(chips):
        to = lax.rem(z + d, chips)
        spread[d] = remote(
            mine.at[pl.ds(pl.multiple_of(to * piece, 8), piece)], slots.at[d],
            spread_send.at[d], spread_recv.at[d], 2 * to + c, b,
        )
        spread[d].start()
    total = mine[pl.ds(pl.multiple_of(z * piece, 8), piece), :]
    for d in near_first(chips):
        spread[d].wait_recv()
        total = total + slots[d]
    full[own(c, z), :] = total
    gather, passed = {}, {}
    for d in far_first(chips):
        gather[d] = remote(
            full.at[own(c, z)], full.at[own(c, z)],
            gather_send.at[d], gather_recv.at[d], 2 * lax.rem(z + d, chips) + c, b,
        )
        gather[d].start()
    for d in [0] + near_first(chips):
        if d:
            gather[d].wait_recv()
        here = own(c, lax.rem(z + chips - d, chips))
        passed[d] = remote(
            full.at[here], full.at[here], pass_send.at[d], pass_recv.at[d], 2 * z + other, b
        )
        passed[d].start()
    for d in [0] + near_first(chips):
        passed[d].wait()
        if d:
            spread[d].wait_send()
            gather[d].wait_send()
    out_ref[...] = full[...]


def chebyshev_mix(rows, per_trait, count, factors, radius):
    shape = (rows, ITERS * TRAITS)
    row = iota(shape, 0)
    lane = iota(shape, 1)
    if per_trait == 8:
        trait = lax.shift_right_logical(row, 3)
    else:
        trait = lax.shift_right_logical(row * 205, 10)
    which = row - trait * per_trait
    degree = lax.shift_right_logical(lane, 4)
    keep = (lane - degree * TRAITS == trait) & (which < LAMBDAS) & (row < count)
    lam = jnp.zeros(shape, F32) + factors[LAMBDAS - 1]
    for k in range(LAMBDAS - 1):
        lam = jnp.where(which == k, factors[k], lam)
    middle = lam + radius
    center = middle / radius
    weight = 1.0 / center
    left = jnp.ones(shape, F32)
    heading = jnp.where(degree == 0, 1.0 / middle, 0.0)
    total = heading
    for sweep in range(1, ITERS):
        left = left * weight
        weight_next = 1.0 / (2.0 * center - weight)
        heading = weight_next * weight * heading + jnp.where(
            degree == sweep, 2.0 * weight_next / radius * left, 0.0
        )
        weight = weight_next
        total = total + heading
    return jnp.where(keep, total, 0.0)


def solve_kernel(
    headcount, full, factors_ref, x_hbm, ridge_ref, pred_ref,
    xs, gram, high, low, basis, rows_scr, x_sem,
):
    load = pltpu.make_async_copy(x_hbm, xs, x_sem)
    load.start()
    for at, (i, j) in enumerate(TILES):
        tile = full[at * TILE:(at + 1) * TILE, :]
        gram[i * TILE:(i + 1) * TILE, j * TILE:(j + 1) * TILE] = tile
        if i != j:
            gram[j * TILE:(j + 1) * TILE, i * TILE:(i + 1) * TILE] = tile.T
    shape = (VARS, VARS)
    eye = iota(shape, 0) == iota(shape, 1)
    parts = range(VARS // TILE)
    average = jnp.concatenate(
        [full[SUMS_AT + j:SUMS_AT + j + 1, :] for j in parts], axis=1
    ) / headcount
    average_col = jnp.sum(
        jnp.where(eye, jnp.broadcast_to(average, shape), 0.0), axis=1, keepdims=True
    )
    diagonal = jnp.where(eye, gram[...], 0.0)
    square = jnp.sum(diagonal, axis=0, keepdims=True)
    square_col = jnp.sum(diagonal, axis=1, keepdims=True)
    inverse = 1.0 / jnp.sqrt(square / headcount - average * average + 1e-05)
    inverse_col = 1.0 / jnp.sqrt(square_col / headcount - average_col * average_col + 1e-05)
    standard = (gram[...] * (1.0 / headcount) - average_col * average) * (inverse_col * inverse)
    limit = jnp.max(jnp.sum(jnp.abs(standard), axis=0, keepdims=True), axis=1, keepdims=True)
    radius = limit / 2.0
    scaled = standard * (1.0 / radius)
    first = scaled.astype(BF16)
    high[...] = first
    low[...] = (scaled - first.astype(F32)).astype(BF16)

    cross = jnp.concatenate(
        [full[CROSS_AT + j * TRAITS:CROSS_AT + (j + 1) * TRAITS, :] for j in parts], axis=1
    )
    small = (TRAITS, TILE)
    trait_col = jnp.sum(
        jnp.where(
            iota(small, 0) == iota(small, 1),
            jnp.broadcast_to(full[TRAIT_AT:TRAIT_AT + 1, :], small), 0.0,
        ),
        axis=1, keepdims=True,
    )
    response = math.sqrt(headcount) * (
        cross / headcount - average * (trait_col / headcount)
    ) * inverse

    def apply(u):
        u_high = u.astype(BF16)
        u_low = (u - u_high.astype(F32)).astype(BF16)
        both = jnp.dot(
            jnp.concatenate([u_high, u_low], axis=0), high[...], preferred_element_type=F32
        )
        return both[:TRAITS] + (
            both[TRAITS:] + jnp.dot(u_high, low[...], preferred_element_type=F32)
        )

    before, now = None, response
    basis[0:TRAITS, :] = now
    for degree in range(1, ITERS):
        step = now - apply(now)
        before, now = now, step if before is None else 2.0 * step - before
        basis[degree * TRAITS:(degree + 1) * TRAITS, :] = now

    factors = [factors_ref[k] for k in range(LAMBDAS)]
    mix = chebyshev_mix(TRAITS * SLOT, SLOT, TRAITS * SLOT, factors, radius)
    solution_rows = jnp.dot(mix, basis[...], precision=HIGHEST, preferred_element_type=F32)
    coef = (solution_rows * (inverse * (1.0 / math.sqrt(VARS)))).astype(BF16)
    offset = jnp.sum(coef.astype(F32) * average, axis=1, keepdims=True)

    count = TRAITS * LAMBDAS
    mix = chebyshev_mix(TILE, LAMBDAS, count, factors, radius)
    packed = jnp.dot(mix, basis[...], precision=HIGHEST, preferred_element_type=F32)
    ridge_ref[...] = packed.T[:, :count]

    load.wait()
    width = xs.shape[0] // PARTS
    for part in range(PARTS):
        predicted = lax.dot_general(
            coef, xs[part * width:(part + 1) * width, :], CONTRACT_LANES,
            preferred_element_type=F32,
        ) - offset
        for t in range(TRAITS):
            rows_scr[t, part * LAMBDAS:(part + 1) * LAMBDAS, :] = predicted[
                t * SLOT:t * SLOT + LAMBDAS, :
            ]
    for t in range(TRAITS):
        pred_ref[t] = rows_scr[t].astype(BF16)


def slot_of(compact):
    block = lax.shift_right_logical(compact * 205, 10)
    return block * SLOT + (compact - block * LAMBDAS)


def level_one_kernel(
    chips, blocks, headcount, pred_ref, y_ref, gram_ref, cross_ref,
    recv, stacked, packed, half, mine, slots, final,
    move_send, move_recv, pair_send, pair_recv, spread_send, spread_recv, pass_send, pass_recv,
):
    z, c, b = position()
    person = 2 * z + c
    other = 1 - c
    for d in range(1, blocks):
        signal(person, lax.rem(b + d, blocks))
    signal(2 * z + other, b)
    for d in range(1, chips):
        signal(2 * lax.rem(z + d, chips) + c, b)

    stacked[...] = jnp.zeros_like(stacked)
    pick = (
        (iota((SLOT, TRAITS), 0) == LAMBDAS) & (iota((SLOT, TRAITS), 1) == b)
    ).astype(F32).astype(BF16)
    trait_row = lax.dot_general(
        pick, y_ref[...], CONTRACT_LANES, preferred_element_type=F32
    )
    pl.semaphore_wait(pltpu.get_barrier_semaphore(), blocks + chips - 1)

    moves = {}
    for d in range(1, blocks):
        to = lax.rem(b + d, blocks)
        moves[d] = remote(
            pred_ref.at[to], recv.at[d], move_send.at[d], move_recv.at[d], person, to
        )
        moves[d].start()
    width = recv.shape[2]

    def place(block, values):
        values = values.astype(F32)
        at = pl.ds(pl.multiple_of(block * SLOT, SLOT), LAMBDAS)
        for part in range(PARTS):
            stacked[at, part * width:(part + 1) * width] = values[
                part * LAMBDAS:(part + 1) * LAMBDAS, :
            ]

    place(b, pred_ref[b])
    for d in range(1, blocks):
        moves[d].wait_recv()
        place(lax.rem(b + blocks - d, blocks), recv[d])
    stacked[LAMBDAS:LAMBDAS + 1, :] = trait_row[LAMBDAS:LAMBDAS + 1, :]

    w = stacked[...].astype(BF16)
    gram = lax.dot_general(w, w, CONTRACT_LANES, preferred_element_type=F32)

    size = blocks * LAMBDAS
    part = size // 2
    square = (TILE, TILE)
    row, lane = iota(square, 0), iota(square, 1)
    cols_a = ((lane < size) & (row == slot_of(lane))) | ((lane == 120) & (row == LAMBDAS))
    cols_b = (
        (lane >= size) & (lane < size + part) & (row == slot_of(lane - part))
    ) | ((lane == 121) & (row == LAMBDAS))
    strip = (packed.shape[0], TILE)
    row, lane = iota(strip, 0), iota(strip, 1)
    rows_a = (row < part) & (lane == slot_of(row))
    rows_b = (row < part) & (lane == slot_of(row + part))

    def select(left, right):
        inner = jnp.dot(
            gram, right.astype(F32), precision=HIGHEST, preferred_element_type=F32
        )
        return jnp.dot(
            left.astype(F32), inner, precision=HIGHEST, preferred_element_type=F32
        )

    packed[...] = select(rows_a, cols_a) + select(rows_b, cols_b)

    rows = packed.shape[0] // 2

    def side(core):
        return pl.ds(pl.multiple_of(core * rows, 8), rows)

    pair = remote(packed.at[side(other)], half, pair_send, pair_recv, 2 * z + other, b)
    pair.start()
    pair.wait()
    mine[...] = packed[side(c), :] + half[...]
    spread = {}
    for d in far_first(chips):
        spread[d] = remote(
            mine, slots.at[z], spread_send.at[d], spread_recv.at[d],
            2 * lax.rem(z + d, chips) + c, b,
        )
        spread[d].start()
    slots[z] = mine[...]
    for d in near_first(chips):
        spread[d].wait_recv()
    total = slots[0]
    for chip in range(1, chips):
        total = total + slots[chip]
    final[side(c), :] = total
    passed = remote(final.at[side(c)], final.at[side(c)], pass_send, pass_recv, 2 * z + other, b)
    passed.start()
    passed.wait()
    for d in range(1, chips):
        spread[d].wait_send()
    for d in range(1, blocks):
        moves[d].wait_send()

    flat = final[...]
    turned = jnp.concatenate(
        [flat, jnp.zeros((TILE - flat.shape[0], TILE), F32)], axis=0
    ).T
    shifted = pltpu.roll(flat, TILE - part, 1)
    lane = iota((part, TILE), 1)
    lower = jnp.where(lane < part, turned[part:size, :], shifted[:part, :])
    gram_ref[0, 0:part, :] = flat[:part, :size] * (1.0 / headcount)
    gram_ref[0, part:size, :] = lower[:, :size] * (1.0 / headcount)
    lane = iota((1, TILE), 1)
    pair_row = jnp.where(lane < part, turned[120:121, :], pltpu.roll(turned[121:122, :], part, 1))
    cross_ref[...] = pair_row[:, :size] * (1.0 / math.sqrt(headcount))


VMEM = pl.BlockSpec(memory_space=pltpu.VMEM)
DMA = pltpu.SemaphoreType.DMA


def per_device(chips, blocks, x, y, factors):
    people = x.shape[0]
    headcount = float(people * chips * 2)
    piece = piece_rows(chips)
    total_rows = 2 * chips * piece
    tile = people // 8
    half = VARS // 2
    partial = pl.pallas_call(
        partial_kernel,
        grid=(people // tile,),
        in_specs=[
            pl.BlockSpec((tile, VARS), lambda i: (i, 0)),
            pl.BlockSpec((tile, TRAITS), lambda i: (i, 0)),
        ],
        out_specs=pl.BlockSpec((total_rows, TILE), lambda i: (0, 0)),
        out_shape=jax.ShapeDtypeStruct((total_rows, TILE), F32),
        scratch_shapes=[
            pltpu.VMEM((half, VARS), F32),
            pltpu.VMEM((half, half), F32),
            pltpu.VMEM((TRAITS, VARS), F32),
            pltpu.VMEM((8, VARS), F32),
            pltpu.VMEM((1, TRAITS), F32),
        ],
        name="partial_sums",
    )(x, y)
    summed = pl.pallas_call(
        functools.partial(people_sum_kernel, chips),
        in_specs=[VMEM],
        out_specs=VMEM,
        out_shape=jax.ShapeDtypeStruct((total_rows, TILE), F32),
        scratch_shapes=[
            pltpu.VMEM((total_rows // 2, TILE), F32),
            pltpu.VMEM((total_rows // 2, TILE), F32),
            pltpu.VMEM((chips, piece, TILE), F32),
            pltpu.VMEM((total_rows, TILE), F32),
            DMA, DMA, DMA((chips,)), DMA((chips,)), DMA((chips,)), DMA((chips,)),
            DMA((chips,)), DMA((chips,)),
        ],
        compiler_params=pltpu.CompilerParams(collective_id=0, has_side_effects=True),
        name="people_sum",
    )(partial)
    width = people // PARTS
    ridge, pred = pl.pallas_call(
        functools.partial(solve_kernel, headcount),
        in_specs=[
            VMEM,
            pl.BlockSpec(memory_space=pltpu.SMEM),
            pl.BlockSpec(memory_space=pl.ANY),
        ],
        out_specs=[VMEM, VMEM],
        out_shape=[
            jax.ShapeDtypeStruct((VARS, TRAITS * LAMBDAS), F32),
            jax.ShapeDtypeStruct((TRAITS, PARTS * LAMBDAS, width), BF16),
        ],
        scratch_shapes=[
            pltpu.VMEM((people, VARS), BF16),
            pltpu.VMEM((VARS, VARS), F32),
            pltpu.VMEM((VARS, VARS), BF16),
            pltpu.VMEM((VARS, VARS), BF16),
            pltpu.VMEM((ITERS * TRAITS, VARS), F32),
            pltpu.VMEM((TRAITS, PARTS * LAMBDAS, width), F32),
            DMA,
        ],
        name="solve",
    )(summed, factors, x)
    size = blocks * LAMBDAS
    rows = 48
    gram, cross = pl.pallas_call(
        functools.partial(level_one_kernel, chips, blocks, headcount),
        in_specs=[VMEM, VMEM],
        out_specs=[VMEM, VMEM],
        out_shape=[
            jax.ShapeDtypeStruct((1, size, size), F32),
            jax.ShapeDtypeStruct((1, size), F32),
        ],
        scratch_shapes=[
            pltpu.VMEM((blocks, PARTS * LAMBDAS, width), BF16),
            pltpu.VMEM((blocks * SLOT, people), F32),
            pltpu.VMEM((rows, TILE), F32),
            pltpu.VMEM((rows // 2, TILE), F32),
            pltpu.VMEM((rows // 2, TILE), F32),
            pltpu.VMEM((chips, rows // 2, TILE), F32),
            pltpu.VMEM((rows, TILE), F32),
            DMA((blocks,)), DMA((blocks,)), DMA, DMA, DMA((chips,)), DMA((chips,)), DMA, DMA,
        ],
        compiler_params=pltpu.CompilerParams(collective_id=1, has_side_effects=True),
        name="level_one",
    )(pred, y)
    return ridge, gram, cross


def solution(mesh):
    chips = mesh.shape["people"] // 2
    return jax.shard_map(
        functools.partial(per_device, chips, mesh.shape["blocks"]),
        mesh=mesh,
        in_specs=(P("people", "blocks"), P("people", None), P()),
        out_specs=(P("blocks", None), P("blocks", None, None), P("blocks", None)),
        check_vma=False,
    )
```

```python
import functools
import math

import jax
import jax.numpy as jnp
from jax import lax
from jax.experimental import pallas as pl
from jax.experimental.pallas import tpu as pltpu
from jax.sharding import PartitionSpec as P

VARS = 512
TRAITS = 16
LAMBDAS = 5
ITERS = 8
SLOT = 8
PARTS = 16
MESH = pl.DeviceIdType.MESH
F32 = jnp.float32
BF16 = jnp.bfloat16
HIGHEST = lax.Precision.HIGHEST

CHUNKS = 8
TILE = 128
EDGE = TILE // 2
STRIPS = VARS // TILE
OFF_TILES = [(i, j) for i in range(STRIPS) for j in range(i + 1, STRIPS)]
UPPER_AT = len(OFF_TILES) * TILE
LOWER_AT = UPPER_AT + STRIPS * EDGE
CROSS_AT = LOWER_AT + STRIPS // 2 * EDGE
SUMS_AT = CROSS_AT + TRAITS * STRIPS
TRAIT_AT = SUMS_AT + STRIPS
USED = SUMS_AT + 8
CONTRACT_ROWS = (((0,), (0,)), ((), ()))
CONTRACT_LANES = (((1,), (1,)), ((), ()))


def piece_rows(chips):
    return -(-USED // (2 * chips * 8)) * 8


def iota(shape, dim):
    return lax.broadcasted_iota(jnp.int32, shape, dim)


def far_first(n):
    return sorted(range(1, n), key=lambda d: -min(d, n - d))


def near_first(n):
    return sorted(range(1, n), key=lambda d: min(d, n - d))


def partial_sums(x_hbm, y_ref, xs, part, top, low, tail, x_sems):
    tile = xs.shape[0] // CHUNKS

    def chunk(i):
        return pl.ds(pl.multiple_of(i * tile, tile), tile)

    def load(i):
        return pltpu.make_async_copy(x_hbm.at[chunk(i)], xs.at[chunk(i)], x_sems.at[i])

    for i in range(CHUNKS):
        load(i).start()
    top[...] = jnp.zeros_like(top)
    low[...] = jnp.zeros_like(low)
    tail[...] = jnp.zeros_like(tail)
    half = VARS // 2

    def step(i, carry):
        load(i).wait()
        x = xs[chunk(i), :]
        lead = jnp.concatenate([y_ref[:, chunk(i)], jnp.ones((TRAITS, tile), BF16)], axis=0)
        top[...] += lax.dot_general(x[:, :half], x, CONTRACT_ROWS, preferred_element_type=F32)
        low[...] += lax.dot_general(
            x[:, half:], x[:, half:], CONTRACT_ROWS, preferred_element_type=F32
        )
        tail[...] += jnp.dot(lead, x, preferred_element_type=F32)
        return carry

    lax.fori_loop(0, CHUNKS, step, 0)

    def tile_of(i, j, first):
        rows, columns = i * TILE + first, j * TILE
        source = top
        if rows >= half:
            source, rows, columns = low, rows - half, columns - half
        return source[rows:(i + 1) * TILE - (half if source is low else 0), columns:columns + TILE]

    for at, (i, j) in enumerate(OFF_TILES):
        part[at * TILE:(at + 1) * TILE, :] = tile_of(i, j, 0)
    left = iota((EDGE, TILE), 1) < EDGE
    for i in range(STRIPS):
        at = UPPER_AT + i * EDGE
        part[at:at + EDGE, :] = tile_of(i, i, 0)[:EDGE]
    for i in range(STRIPS // 2):
        at = LOWER_AT + i * EDGE
        part[at:at + EDGE, :] = jnp.where(
            left, pltpu.roll(tile_of(2 * i, 2 * i, EDGE), EDGE, 1),
            tile_of(2 * i + 1, 2 * i + 1, EDGE),
        )
    for j in range(STRIPS):
        at = CROSS_AT + j * TRAITS
        part[at:at + TRAITS, :] = tail[0:TRAITS, j * TILE:(j + 1) * TILE]
    part[SUMS_AT:, :] = jnp.zeros((part.shape[0] - SUMS_AT, TILE), F32)
    for j in range(STRIPS):
        part[SUMS_AT + j:SUMS_AT + j + 1, :] = tail[
            TRAITS:TRAITS + 1, j * TILE:(j + 1) * TILE
        ]
    trait = jnp.sum(y_ref[...].astype(F32), axis=1, keepdims=True)
    small = (TRAITS, TILE)
    part[TRAIT_AT:TRAIT_AT + 1, :] = jnp.sum(
        jnp.where(iota(small, 0) == iota(small, 1), jnp.broadcast_to(trait, small), 0.0),
        axis=0, keepdims=True,
    )


def position():
    person = lax.axis_index("people")
    return lax.div(person, 2), lax.rem(person, 2), lax.axis_index("blocks")


def remote(src, dst, send, recv, people, block):
    return pltpu.make_async_remote_copy(
        src_ref=src, dst_ref=dst, send_sem=send, recv_sem=recv,
        device_id=(people, block), device_id_type=MESH,
    )


def signal(people, block):
    pl.semaphore_signal(
        pltpu.get_barrier_semaphore(), inc=1, device_id=(people, block), device_id_type=MESH
    )


def people_sum(chips, part, full, half, mine, other_half, ours, slots, sems):
    (
        pair_send, pair_recv, near_send, near_recv, spread_send, spread_recv,
        gather_send, gather_recv, near_back_send, near_back_recv, pass_send, pass_recv,
    ) = sems
    z, c, b = position()
    other = 1 - c
    odd, place = lax.rem(z, 2), lax.div(z, 2)
    peers = chips // 2
    near = lax.rem(z + (1 - 2 * odd) * (1 - 2 * c) + chips, chips)
    piece = slots.shape[1]
    rows = chips * piece
    side = peers * piece

    def rows_at(start, count):
        return pl.ds(pl.multiple_of(start, 8), count)

    pair = remote(
        part.at[rows_at(other * rows, rows)], half, pair_send, pair_recv, 2 * z + other, b
    )
    pair.start()
    pair.wait()
    mine[...] = part[rows_at(c * rows, rows), :] + half[...]
    swap = remote(
        mine.at[rows_at((1 - odd) * side, side)], other_half,
        near_send, near_recv, 2 * near + c, b,
    )
    swap.start()
    swap.wait()
    ours[...] = mine[rows_at(odd * side, side), :] + other_half[...]
    spread = {}
    for d in far_first(peers):
        to = lax.rem(place + d, peers)
        spread[d] = remote(
            ours.at[rows_at(to * piece, piece)], slots.at[d],
            spread_send.at[d], spread_recv.at[d], 2 * (2 * to + odd) + c, b,
        )
        spread[d].start()
    total = ours[rows_at(place * piece, piece), :]
    for d in near_first(peers):
        spread[d].wait_recv()
        total = total + slots[d]

    def own(parity, at):
        return rows_at(c * rows + parity * side + at * piece, piece)

    full[own(odd, place), :] = total
    here = own(odd, place)
    gather = {}
    for d in far_first(peers):
        to = 2 * (2 * lax.rem(place + d, peers) + odd) + c
        gather[d] = remote(
            full.at[here], full.at[here], gather_send.at[d], gather_recv.at[d], to, b
        )
        gather[d].start()
    back, passed = {}, {}
    for d in [0] + near_first(peers):
        if d:
            gather[d].wait_recv()
        here = own(odd, lax.rem(place + peers - d, peers))
        back[d] = remote(
            full.at[here], full.at[here], near_back_send.at[d], near_back_recv.at[d],
            2 * near + c, b,
        )
        back[d].start()
        passed[d] = remote(
            full.at[here], full.at[here], pass_send.at[d], pass_recv.at[d], 2 * z + other, b
        )
        passed[d].start()
    near_place = lax.div(near, 2)
    for d in [0] + near_first(peers):
        back[d].wait_recv()
        here = own(1 - odd, lax.rem(near_place + peers - d, peers))
        passed[peers + d] = remote(
            full.at[here], full.at[here], pass_send.at[peers + d], pass_recv.at[peers + d],
            2 * z + other, b,
        )
        passed[peers + d].start()
    for copy in passed.values():
        copy.wait()
    for d in range(peers):
        back[d].wait_send()
        if d:
            spread[d].wait_send()
            gather[d].wait_send()


def chebyshev_mix(rows, per_trait, count, factors, radius):
    shape = (rows, ITERS * TRAITS)
    row = iota(shape, 0)
    lane = iota(shape, 1)
    if per_trait == 8:
        trait = lax.shift_right_logical(row, 3)
    else:
        trait = lax.shift_right_logical(row * 205, 10)
    which = row - trait * per_trait
    degree = lax.shift_right_logical(lane, 4)
    keep = (lane - degree * TRAITS == trait) & (which < LAMBDAS) & (row < count)
    lam = jnp.zeros(shape, F32) + factors[LAMBDAS - 1]
    for k in range(LAMBDAS - 1):
        lam = jnp.where(which == k, factors[k], lam)
    middle = lam + radius
    center = middle / radius
    weight = 1.0 / center
    left = jnp.ones(shape, F32)
    heading = jnp.where(degree == 0, 1.0 / middle, 0.0)
    total = heading
    for sweep in range(1, ITERS):
        left = left * weight
        weight_next = 1.0 / (2.0 * center - weight)
        heading = weight_next * weight * heading + jnp.where(
            degree == sweep, 2.0 * weight_next / radius * left, 0.0
        )
        weight = weight_next
        total = total + heading
    return jnp.where(keep, total, 0.0)


def solve(headcount, full, factors_ref, xs, pred, gram, high, low, basis, rows_scr):
    for at, (i, j) in enumerate(OFF_TILES):
        tile = full[at * TILE:(at + 1) * TILE, :]
        gram[i * TILE:(i + 1) * TILE, j * TILE:(j + 1) * TILE] = tile
        gram[j * TILE:(j + 1) * TILE, i * TILE:(i + 1) * TILE] = tile.T
    left = iota((EDGE, TILE), 1) < EDGE
    for i in range(STRIPS):
        upper = full[UPPER_AT + i * EDGE:UPPER_AT + (i + 1) * EDGE, :]
        at = LOWER_AT + i // 2 * EDGE
        lower = full[at:at + EDGE, :]
        if i % 2 == 0:
            lower = pltpu.roll(lower, EDGE, 1)
        turned = jnp.concatenate([upper, jnp.zeros((EDGE, TILE), F32)], axis=0).T
        columns = slice(i * TILE, (i + 1) * TILE)
        gram[i * TILE:i * TILE + EDGE, columns] = upper
        gram[i * TILE + EDGE:(i + 1) * TILE, columns] = jnp.where(left, turned[EDGE:, :], lower)
    shape = (VARS, VARS)
    eye = iota(shape, 0) == iota(shape, 1)
    parts = range(VARS // TILE)
    average = jnp.concatenate(
        [full[SUMS_AT + j:SUMS_AT + j + 1, :] for j in parts], axis=1
    ) / headcount
    average_col = jnp.sum(
        jnp.where(eye, jnp.broadcast_to(average, shape), 0.0), axis=1, keepdims=True
    )
    diagonal = jnp.where(eye, gram[...], 0.0)
    square = jnp.sum(diagonal, axis=0, keepdims=True)
    square_col = jnp.sum(diagonal, axis=1, keepdims=True)
    inverse = 1.0 / jnp.sqrt(square / headcount - average * average + 1e-05)
    inverse_col = 1.0 / jnp.sqrt(square_col / headcount - average_col * average_col + 1e-05)
    standard = (gram[...] * (1.0 / headcount) - average_col * average) * (inverse_col * inverse)
    limit = jnp.max(jnp.sum(jnp.abs(standard), axis=0, keepdims=True), axis=1, keepdims=True)
    radius = limit / 2.0
    scaled = standard * (1.0 / radius)
    first = scaled.astype(BF16)
    high[...] = first
    low[...] = (scaled - first.astype(F32)).astype(BF16)

    cross = jnp.concatenate(
        [full[CROSS_AT + j * TRAITS:CROSS_AT + (j + 1) * TRAITS, :] for j in parts], axis=1
    )
    small = (TRAITS, TILE)
    trait_col = jnp.sum(
        jnp.where(
            iota(small, 0) == iota(small, 1),
            jnp.broadcast_to(full[TRAIT_AT:TRAIT_AT + 1, :], small), 0.0,
        ),
        axis=1, keepdims=True,
    )
    response = math.sqrt(headcount) * (
        cross / headcount - average * (trait_col / headcount)
    ) * inverse

    def apply(u):
        u_high = u.astype(BF16)
        u_low = (u - u_high.astype(F32)).astype(BF16)
        both = jnp.dot(
            jnp.concatenate([u_high, u_low], axis=0), high[...], preferred_element_type=F32
        )
        return both[:TRAITS] + (
            both[TRAITS:] + jnp.dot(u_high, low[...], preferred_element_type=F32)
        )

    before, now = None, response
    basis[0:TRAITS, :] = now
    for degree in range(1, ITERS):
        step = now - apply(now)
        before, now = now, step if before is None else 2.0 * step - before
        basis[degree * TRAITS:(degree + 1) * TRAITS, :] = now

    factors = [factors_ref[k] for k in range(LAMBDAS)]
    mix = chebyshev_mix(TRAITS * SLOT, SLOT, TRAITS * SLOT, factors, radius)
    solution_rows = jnp.dot(mix, basis[...], precision=HIGHEST, preferred_element_type=F32)
    coef = (solution_rows * (inverse * (1.0 / math.sqrt(VARS)))).astype(BF16)
    offset = jnp.sum(coef.astype(F32) * average, axis=1, keepdims=True)

    width = xs.shape[0] // PARTS
    for part in range(PARTS):
        predicted = lax.dot_general(
            coef, xs[part * width:(part + 1) * width, :], CONTRACT_LANES,
            preferred_element_type=F32,
        ) - offset
        for t in range(TRAITS):
            rows_scr[t, part * LAMBDAS:(part + 1) * LAMBDAS, :] = predicted[
                t * SLOT:t * SLOT + LAMBDAS, :
            ]
    for t in range(TRAITS):
        pred[t] = rows_scr[t].astype(BF16)
    return factors, radius


def slot_of(compact):
    block = lax.shift_right_logical(compact * 205, 10)
    return block * SLOT + (compact - block * LAMBDAS)


def whole_kernel(
    chips, blocks, headcount, y_ref, factors_ref, x_hbm, ridge_ref, final_ref,
    xs, part, top, low, tail, full, half, mine, other_half, ours, slots,
    gram_scr, high, low_part, basis, rows_scr, pred, recv, stacked,
    packed, last_half, last_mine, last_slots, final,
    x_sems, *sems,
):
    z, c, b = position()
    person = 2 * z + c
    other = 1 - c
    for d in range(1, chips):
        signal(2 * lax.rem(z + d, chips) + c, b)
    signal(2 * z + other, b)
    for d in range(1, blocks):
        signal(person, lax.rem(b + d, blocks))

    partial_sums(x_hbm, y_ref, xs, part, top, low, tail, x_sems)
    stacked[...] = jnp.zeros_like(stacked)
    pl.semaphore_wait(pltpu.get_barrier_semaphore(), blocks + chips - 1)
    people_sum(chips, part, full, half, mine, other_half, ours, slots, sems[:12])
    factors, radius = solve(
        headcount, full, factors_ref, xs, pred, gram_scr, high, low_part, basis, rows_scr
    )

    (
        move_send, move_recv, pair_send, pair_recv, spread_send, spread_recv, pass_send, pass_recv,
    ) = sems[12:]
    moves = {}
    for d in range(1, blocks):
        to = lax.rem(b + d, blocks)
        moves[d] = remote(
            pred.at[to], recv.at[d], move_send.at[d], move_recv.at[d], person, to
        )
        moves[d].start()

    count = TRAITS * LAMBDAS
    mix = chebyshev_mix(count, LAMBDAS, count, factors, radius)
    ridge_ref[...] = jnp.dot(mix, basis[...], precision=HIGHEST, preferred_element_type=F32)
    pick = (
        (iota((SLOT, TRAITS), 0) == LAMBDAS) & (iota((SLOT, TRAITS), 1) == b)
    ).astype(F32).astype(BF16)
    trait_row = jnp.dot(pick, y_ref[...], preferred_element_type=F32)
    width = recv.shape[2]

    def place(block, values):
        values = values.astype(F32)
        at = pl.ds(pl.multiple_of(block * SLOT, SLOT), LAMBDAS)
        for part in range(PARTS):
            stacked[at, part * width:(part + 1) * width] = values[
                part * LAMBDAS:(part + 1) * LAMBDAS, :
            ]

    place(b, pred[b])
    for d in range(1, blocks):
        moves[d].wait_recv()
        place(lax.rem(b + blocks - d, blocks), recv[d])
    stacked[LAMBDAS:LAMBDAS + 1, :] = trait_row[LAMBDAS:LAMBDAS + 1, :]

    w = stacked[...].astype(BF16)
    gram = lax.dot_general(w, w, CONTRACT_LANES, preferred_element_type=F32)

    size = blocks * LAMBDAS
    part = size // 2
    square = (TILE, TILE)
    row, lane = iota(square, 0), iota(square, 1)
    cols_a = ((lane < size) & (row == slot_of(lane))) | ((lane == 120) & (row == LAMBDAS))
    cols_b = (
        (lane >= size) & (lane < size + part) & (row == slot_of(lane - part))
    ) | ((lane == 121) & (row == LAMBDAS))
    strip = (packed.shape[0], TILE)
    row, lane = iota(strip, 0), iota(strip, 1)
    rows_a = (row < part) & (lane == slot_of(row))
    rows_b = (row < part) & (lane == slot_of(row + part))

    def select(left, right):
        inner = jnp.dot(
            gram, right.astype(F32), precision=HIGHEST, preferred_element_type=F32
        )
        return jnp.dot(
            left.astype(F32), inner, precision=HIGHEST, preferred_element_type=F32
        )

    packed[...] = select(rows_a, cols_a) + select(rows_b, cols_b)

    rows = packed.shape[0] // 2

    def side(core):
        return pl.ds(pl.multiple_of(core * rows, 8), rows)

    pair = remote(packed.at[side(other)], last_half, pair_send, pair_recv, 2 * z + other, b)
    pair.start()
    pair.wait()
    last_mine[...] = packed[side(c), :] + last_half[...]
    spread = {}
    for d in far_first(chips):
        spread[d] = remote(
            last_mine, last_slots.at[z], spread_send.at[d], spread_recv.at[d],
            2 * lax.rem(z + d, chips) + c, b,
        )
        spread[d].start()
    last_slots[z] = last_mine[...]
    for d in near_first(chips):
        spread[d].wait_recv()
    total = last_slots[0]
    for chip in range(1, chips):
        total = total + last_slots[chip]
    final[side(c), :] = total
    passed = remote(final.at[side(c)], final.at[side(c)], pass_send, pass_recv, 2 * z + other, b)
    passed.start()
    passed.wait()
    for d in range(1, chips):
        spread[d].wait_send()
    for d in range(1, blocks):
        moves[d].wait_send()

    final_ref[...] = final[...]


def finish_kernel(size, headcount, rows_ref, flat_ref, ridge_ref, gram_ref, cross_ref):
    ridge_ref[...] = rows_ref[...]
    part = size // 2
    flat = flat_ref[...]
    turned = jnp.concatenate(
        [flat, jnp.zeros((TILE - flat.shape[0], TILE), F32)], axis=0
    ).T
    shifted = pltpu.roll(flat, TILE - part, 1)
    lane = iota((part, TILE), 1)
    lower = jnp.where(lane < part, turned[part:size, :], shifted[:part, :])
    gram_ref[0, 0:part, :] = flat[:part, :size] * (1.0 / headcount)
    gram_ref[0, part:size, :] = lower[:, :size] * (1.0 / headcount)
    lane = iota((1, TILE), 1)
    pair_row = jnp.where(lane < part, turned[120:121, :], pltpu.roll(turned[121:122, :], part, 1))
    cross_ref[...] = pair_row[:, :size] * (1.0 / math.sqrt(headcount))


VMEM = pl.BlockSpec(memory_space=pltpu.VMEM)
DMA = pltpu.SemaphoreType.DMA


def per_device(chips, blocks, x, y, factors):
    people = x.shape[0]
    headcount = float(people * chips * 2)
    piece = piece_rows(chips)
    total_rows = 2 * chips * piece
    core_rows = chips * piece
    peers = chips // 2
    half = VARS // 2
    width = people // PARTS
    size = blocks * LAMBDAS
    rows = 48
    rows_shape = jax.ShapeDtypeStruct((TRAITS * LAMBDAS, VARS), F32)
    ridge, final = pl.pallas_call(
        functools.partial(whole_kernel, chips, blocks, headcount),
        in_specs=[
            VMEM,
            pl.BlockSpec(memory_space=pltpu.SMEM),
            pl.BlockSpec(memory_space=pl.ANY),
        ],
        out_specs=[VMEM, VMEM],
        out_shape=[rows_shape, jax.ShapeDtypeStruct((rows, TILE), F32)],
        scratch_shapes=[
            pltpu.VMEM((people, VARS), BF16),
            pltpu.VMEM((total_rows, TILE), F32),
            pltpu.VMEM((half, VARS), F32),
            pltpu.VMEM((half, half), F32),
            pltpu.VMEM((2 * TRAITS, VARS), F32),
            pltpu.VMEM((total_rows, TILE), F32),
            pltpu.VMEM((core_rows, TILE), F32),
            pltpu.VMEM((core_rows, TILE), F32),
            pltpu.VMEM((core_rows // 2, TILE), F32),
            pltpu.VMEM((core_rows // 2, TILE), F32),
            pltpu.VMEM((peers, piece, TILE), F32),
            pltpu.VMEM((VARS, VARS), F32),
            pltpu.VMEM((VARS, VARS), BF16),
            pltpu.VMEM((VARS, VARS), BF16),
            pltpu.VMEM((ITERS * TRAITS, VARS), F32),
            pltpu.VMEM((TRAITS, PARTS * LAMBDAS, width), F32),
            pltpu.VMEM((TRAITS, PARTS * LAMBDAS, width), BF16),
            pltpu.VMEM((blocks, PARTS * LAMBDAS, width), BF16),
            pltpu.VMEM((blocks * SLOT, people), F32),
            pltpu.VMEM((rows, TILE), F32),
            pltpu.VMEM((rows // 2, TILE), F32),
            pltpu.VMEM((rows // 2, TILE), F32),
            pltpu.VMEM((chips, rows // 2, TILE), F32),
            pltpu.VMEM((rows, TILE), F32),
            DMA((CHUNKS,)),
            DMA, DMA, DMA, DMA, DMA((peers,)), DMA((peers,)), DMA((peers,)), DMA((peers,)),
            DMA((peers,)), DMA((peers,)), DMA((chips,)), DMA((chips,)),
            DMA((blocks,)), DMA((blocks,)), DMA, DMA, DMA((chips,)), DMA((chips,)), DMA, DMA,
        ],
        compiler_params=pltpu.CompilerParams(collective_id=0, has_side_effects=True),
        name="whole",
    )(y.T, factors, x)
    ridge, gram, cross = pl.pallas_call(
        functools.partial(finish_kernel, size, headcount),
        in_specs=[VMEM, VMEM],
        out_specs=[VMEM, VMEM, VMEM],
        out_shape=[
            rows_shape,
            jax.ShapeDtypeStruct((1, size, size), F32),
            jax.ShapeDtypeStruct((1, size), F32),
        ],
        name="finish",
    )(ridge, final)
    return ridge.T, gram, cross


def solution(mesh):
    chips = mesh.shape["people"] // 2
    return jax.shard_map(
        functools.partial(per_device, chips, mesh.shape["blocks"]),
        mesh=mesh,
        in_specs=(P("people", "blocks"), P("people", None), P()),
        out_specs=(P("blocks", None), P("blocks", None, None), P("blocks", None)),
        check_vma=False,
    )
```

```python
import functools
import math

import jax
import jax.numpy as jnp
from jax import lax
from jax.experimental import pallas as pl
from jax.experimental.pallas import tpu as pltpu
from jax.sharding import PartitionSpec as P

VARS = 512
TRAITS = 16
LAMBDAS = 5
ITERS = 8
SLOT = 8
PARTS = 16
MESH = pl.DeviceIdType.MESH
F32 = jnp.float32
BF16 = jnp.bfloat16
HIGHEST = lax.Precision.HIGHEST

CHUNKS = 8
TILE = 128
EDGE = TILE // 2
STRIPS = VARS // TILE
OFF_AT = {(0, 1): 0, (0, 2): 128, (0, 3): 256, (1, 2): 384, (1, 3): 512, (2, 3): 768}
UPPER_AT = (640, 704, 896, 960)
LOWER_AT = (1024, 1088)
CROSS_AT = 1152
SUMS_AT = CROSS_AT + TRAITS * STRIPS
TRAIT_AT = SUMS_AT + STRIPS
SETS = ((0, 768), (768, 512))
TOTAL_ROWS = 1280
CONTRACT_ROWS = (((0,), (0,)), ((), ()))
CONTRACT_LANES = (((1,), (1,)), ((), ()))


def iota(shape, dim):
    return lax.broadcasted_iota(jnp.int32, shape, dim)


def far_first(n):
    return sorted(range(1, n), key=lambda d: -min(d, n - d))


def near_first(n):
    return sorted(range(1, n), key=lambda d: min(d, n - d))


def loads(x_hbm, xs, x_sems):
    tile = xs.shape[0] // CHUNKS

    def chunk(i):
        return pl.ds(pl.multiple_of(i * tile, tile), tile)

    def load(i):
        return pltpu.make_async_copy(x_hbm.at[chunk(i)], xs.at[chunk(i)], x_sems.at[i])

    return chunk, load


def first_sums(x_hbm, xs, part, top, x_sems):
    chunk, load = loads(x_hbm, xs, x_sems)
    half = VARS // 2
    top[...] = jnp.zeros_like(top)

    def step(i, carry):
        load(i).wait()
        x = xs[chunk(i), :]
        top[...] += lax.dot_general(x[:, :half], x, CONTRACT_ROWS, preferred_element_type=F32)
        return carry

    lax.fori_loop(0, CHUNKS, step, 0)
    for (i, j), at in OFF_AT.items():
        if i < STRIPS // 2:
            part[at:at + TILE, :] = top[i * TILE:(i + 1) * TILE, j * TILE:(j + 1) * TILE]
    for i in range(STRIPS // 2):
        at, corner = UPPER_AT[i], i * TILE
        part[at:at + EDGE, :] = top[corner:corner + EDGE, corner:corner + TILE]


def second_sums(y_ref, xs, part, top, low, tail):
    chunk, _ = loads(None, xs, None)
    tile = xs.shape[0] // CHUNKS
    half = VARS // 2
    low[...] = jnp.zeros_like(low)
    tail[...] = jnp.zeros_like(tail)

    def step(i, carry):
        x = xs[chunk(i), :]
        lead = jnp.concatenate([y_ref[:, chunk(i)], jnp.ones((TRAITS, tile), BF16)], axis=0)
        low[...] += lax.dot_general(
            x[:, half:], x[:, half:], CONTRACT_ROWS, preferred_element_type=F32
        )
        tail[...] += jnp.dot(lead, x, preferred_element_type=F32)
        return carry

    lax.fori_loop(0, CHUNKS, step, 0)
    left = iota((EDGE, TILE), 1) < EDGE
    at = OFF_AT[2, 3]
    part[at:at + TILE, :] = low[:TILE, TILE:]
    for i in range(2):
        at, corner = UPPER_AT[2 + i], i * TILE
        part[at:at + EDGE, :] = low[corner:corner + EDGE, corner:corner + TILE]
    for at, source in zip(LOWER_AT, (top, low)):
        part[at:at + EDGE, :] = jnp.where(
            left, pltpu.roll(source[EDGE:TILE, :TILE], EDGE, 1),
            source[TILE + EDGE:2 * TILE, TILE:2 * TILE],
        )
    for j in range(STRIPS):
        at = CROSS_AT + j * TRAITS
        part[at:at + TRAITS, :] = tail[0:TRAITS, j * TILE:(j + 1) * TILE]
    part[SUMS_AT:, :] = jnp.zeros((TOTAL_ROWS - SUMS_AT, TILE), F32)
    for j in range(STRIPS):
        part[SUMS_AT + j:SUMS_AT + j + 1, :] = tail[
            TRAITS:TRAITS + 1, j * TILE:(j + 1) * TILE
        ]
    trait = jnp.sum(y_ref[...].astype(F32), axis=1, keepdims=True)
    small = (TRAITS, TILE)
    part[TRAIT_AT:TRAIT_AT + 1, :] = jnp.sum(
        jnp.where(iota(small, 0) == iota(small, 1), jnp.broadcast_to(trait, small), 0.0),
        axis=0, keepdims=True,
    )


def position():
    person = lax.axis_index("people")
    return lax.div(person, 2), lax.rem(person, 2), lax.axis_index("blocks")


def remote(src, dst, send, recv, people, block):
    return pltpu.make_async_remote_copy(
        src_ref=src, dst_ref=dst, send_sem=send, recv_sem=recv,
        device_id=(people, block), device_id_type=MESH,
    )


def signal(people, block):
    pl.semaphore_signal(
        pltpu.get_barrier_semaphore(), inc=1, device_id=(people, block), device_id_type=MESH
    )


def people_sum(chips, base, part, full, half, mine, other_half, ours, slots, sems):
    (
        pair_send, pair_recv, near_send, near_recv, spread_send, spread_recv,
        gather_send, gather_recv, near_back_send, near_back_recv, pass_send, pass_recv,
    ) = sems
    z, c, b = position()
    other = 1 - c
    odd, place = lax.rem(z, 2), lax.div(z, 2)
    peers = chips // 2
    near = lax.rem(z + (1 - 2 * odd) * (1 - 2 * c) + chips, chips)
    piece = slots.shape[1]
    rows = chips * piece
    side = peers * piece

    def rows_at(start, count):
        return pl.ds(pl.multiple_of(start, 8), count)

    pair = remote(
        part.at[rows_at(base + other * rows, rows)], half, pair_send, pair_recv, 2 * z + other, b
    )
    pair.start()
    yield
    pair.wait()
    mine[...] = part[rows_at(base + c * rows, rows), :] + half[...]
    swap = remote(
        mine.at[rows_at((1 - odd) * side, side)], other_half,
        near_send, near_recv, 2 * near + c, b,
    )
    swap.start()
    yield
    swap.wait()
    ours[...] = mine[rows_at(odd * side, side), :] + other_half[...]
    spread = {}
    for d in far_first(peers):
        to = lax.rem(place + d, peers)
        spread[d] = remote(
            ours.at[rows_at(to * piece, piece)], slots.at[d],
            spread_send.at[d], spread_recv.at[d], 2 * (2 * to + odd) + c, b,
        )
        spread[d].start()
    yield
    total = ours[rows_at(place * piece, piece), :]
    for d in near_first(peers):
        spread[d].wait_recv()
        total = total + slots[d]

    def own(parity, at):
        return rows_at(base + c * rows + parity * side + at * piece, piece)

    full[own(odd, place), :] = total
    here = own(odd, place)
    gather = {}
    for d in far_first(peers):
        to = 2 * (2 * lax.rem(place + d, peers) + odd) + c
        gather[d] = remote(
            full.at[here], full.at[here], gather_send.at[d], gather_recv.at[d], to, b
        )
        gather[d].start()
    yield
    back, passed = {}, {}
    for d in [0] + near_first(peers):
        if d:
            gather[d].wait_recv()
        here = own(odd, lax.rem(place + peers - d, peers))
        back[d] = remote(
            full.at[here], full.at[here], near_back_send.at[d], near_back_recv.at[d],
            2 * near + c, b,
        )
        back[d].start()
        passed[d] = remote(
            full.at[here], full.at[here], pass_send.at[d], pass_recv.at[d], 2 * z + other, b
        )
        passed[d].start()
    yield
    near_place = lax.div(near, 2)
    for d in [0] + near_first(peers):
        back[d].wait_recv()
        here = own(1 - odd, lax.rem(near_place + peers - d, peers))
        passed[peers + d] = remote(
            full.at[here], full.at[here], pass_send.at[peers + d], pass_recv.at[peers + d],
            2 * z + other, b,
        )
        passed[peers + d].start()
    yield
    for copy in passed.values():
        copy.wait()
    for d in range(peers):
        back[d].wait_send()
        if d:
            spread[d].wait_send()
            gather[d].wait_send()


def chebyshev_mix(rows, per_trait, count, factors, radius):
    shape = (rows, ITERS * TRAITS)
    row = iota(shape, 0)
    lane = iota(shape, 1)
    if per_trait == 8:
        trait = lax.shift_right_logical(row, 3)
    else:
        trait = lax.shift_right_logical(row * 205, 10)
    which = row - trait * per_trait
    degree = lax.shift_right_logical(lane, 4)
    keep = (lane - degree * TRAITS == trait) & (which < LAMBDAS) & (row < count)
    lam = jnp.zeros(shape, F32) + factors[LAMBDAS - 1]
    for k in range(LAMBDAS - 1):
        lam = jnp.where(which == k, factors[k], lam)
    middle = lam + radius
    center = middle / radius
    weight = 1.0 / center
    left = jnp.ones(shape, F32)
    heading = jnp.where(degree == 0, 1.0 / middle, 0.0)
    total = heading
    for sweep in range(1, ITERS):
        left = left * weight
        weight_next = 1.0 / (2.0 * center - weight)
        heading = weight_next * weight * heading + jnp.where(
            degree == sweep, 2.0 * weight_next / radius * left, 0.0
        )
        weight = weight_next
        total = total + heading
    return jnp.where(keep, total, 0.0)


def solve(headcount, full, factors_ref, xs, pred, gram, high, low, basis, rows_scr):
    for (i, j), at in OFF_AT.items():
        tile = full[at:at + TILE, :]
        gram[i * TILE:(i + 1) * TILE, j * TILE:(j + 1) * TILE] = tile
        gram[j * TILE:(j + 1) * TILE, i * TILE:(i + 1) * TILE] = tile.T
    left = iota((EDGE, TILE), 1) < EDGE
    for i in range(STRIPS):
        upper = full[UPPER_AT[i]:UPPER_AT[i] + EDGE, :]
        at = LOWER_AT[i // 2]
        lower = full[at:at + EDGE, :]
        if i % 2 == 0:
            lower = pltpu.roll(lower, EDGE, 1)
        turned = jnp.concatenate([upper, jnp.zeros((EDGE, TILE), F32)], axis=0).T
        columns = slice(i * TILE, (i + 1) * TILE)
        gram[i * TILE:i * TILE + EDGE, columns] = upper
        gram[i * TILE + EDGE:(i + 1) * TILE, columns] = jnp.where(left, turned[EDGE:, :], lower)
    shape = (VARS, VARS)
    eye = iota(shape, 0) == iota(shape, 1)
    parts = range(VARS // TILE)
    average = jnp.concatenate(
        [full[SUMS_AT + j:SUMS_AT + j + 1, :] for j in parts], axis=1
    ) / headcount
    average_col = jnp.sum(
        jnp.where(eye, jnp.broadcast_to(average, shape), 0.0), axis=1, keepdims=True
    )
    diagonal = jnp.where(eye, gram[...], 0.0)
    square = jnp.sum(diagonal, axis=0, keepdims=True)
    square_col = jnp.sum(diagonal, axis=1, keepdims=True)
    inverse = 1.0 / jnp.sqrt(square / headcount - average * average + 1e-05)
    inverse_col = 1.0 / jnp.sqrt(square_col / headcount - average_col * average_col + 1e-05)
    standard = (gram[...] * (1.0 / headcount) - average_col * average) * (inverse_col * inverse)
    limit = jnp.max(jnp.sum(jnp.abs(standard), axis=0, keepdims=True), axis=1, keepdims=True)
    radius = limit / 2.0
    scaled = standard * (1.0 / radius)
    first = scaled.astype(BF16)
    high[...] = first
    low[...] = (scaled - first.astype(F32)).astype(BF16)

    cross = jnp.concatenate(
        [full[CROSS_AT + j * TRAITS:CROSS_AT + (j + 1) * TRAITS, :] for j in parts], axis=1
    )
    small = (TRAITS, TILE)
    trait_col = jnp.sum(
        jnp.where(
            iota(small, 0) == iota(small, 1),
            jnp.broadcast_to(full[TRAIT_AT:TRAIT_AT + 1, :], small), 0.0,
        ),
        axis=1, keepdims=True,
    )
    response = math.sqrt(headcount) * (
        cross / headcount - average * (trait_col / headcount)
    ) * inverse

    def apply(u):
        u_high = u.astype(BF16)
        u_low = (u - u_high.astype(F32)).astype(BF16)
        both = jnp.dot(
            jnp.concatenate([u_high, u_low], axis=0), high[...], preferred_element_type=F32
        )
        return both[:TRAITS] + (
            both[TRAITS:] + jnp.dot(u_high, low[...], preferred_element_type=F32)
        )

    before, now = None, response
    basis[0:TRAITS, :] = now
    for degree in range(1, ITERS):
        step = now - apply(now)
        before, now = now, step if before is None else 2.0 * step - before
        basis[degree * TRAITS:(degree + 1) * TRAITS, :] = now

    factors = [factors_ref[k] for k in range(LAMBDAS)]
    mix = chebyshev_mix(TRAITS * SLOT, SLOT, TRAITS * SLOT, factors, radius)
    solution_rows = jnp.dot(mix, basis[...], precision=HIGHEST, preferred_element_type=F32)
    coef = (solution_rows * (inverse * (1.0 / math.sqrt(VARS)))).astype(BF16)
    offset = jnp.sum(coef.astype(F32) * average, axis=1, keepdims=True)

    width = xs.shape[0] // PARTS
    for part in range(PARTS):
        predicted = lax.dot_general(
            coef, xs[part * width:(part + 1) * width, :], CONTRACT_LANES,
            preferred_element_type=F32,
        ) - offset
        for t in range(TRAITS):
            rows_scr[t, part * LAMBDAS:(part + 1) * LAMBDAS, :] = predicted[
                t * SLOT:t * SLOT + LAMBDAS, :
            ]
    for t in range(TRAITS):
        pred[t] = rows_scr[t].astype(BF16)
    return factors, radius


def slot_of(compact):
    block = lax.shift_right_logical(compact * 205, 10)
    return block * SLOT + (compact - block * LAMBDAS)


def whole_kernel(
    chips, blocks, headcount, y_ref, factors_ref, x_hbm, ridge_ref, final_ref,
    xs, part, top, low, tail, full, *rest,
):
    buffers, rest = (rest[0:5], rest[5:10]), rest[10:]
    gram_scr, high, low_part, basis, rows_scr, pred, recv, stacked = rest[:8]
    packed, last_half, last_mine, last_slots, final, x_sems = rest[8:14]
    sems = rest[14:]
    _, load = loads(x_hbm, xs, x_sems)
    for i in range(CHUNKS):
        load(i).start()
    z, c, b = position()
    person = 2 * z + c
    other = 1 - c
    for d in range(1, chips):
        signal(2 * lax.rem(z + d, chips) + c, b)
    signal(2 * z + other, b)
    for d in range(1, blocks):
        signal(person, lax.rem(b + d, blocks))

    first_sums(x_hbm, xs, part, top, x_sems)
    pl.semaphore_wait(pltpu.get_barrier_semaphore(), blocks + chips - 1)
    stages = [
        people_sum(chips, base, part, full, *buffers[at], sems[12 * at:12 * at + 12])
        for at, (base, _) in enumerate(SETS)
    ]
    next(stages[0])
    second_sums(y_ref, xs, part, top, low, tail)
    stacked[...] = jnp.zeros_like(stacked)
    next(stages[1])
    for _ in range(6):
        for stage in stages:
            next(stage, None)
    factors, radius = solve(
        headcount, full, factors_ref, xs, pred, gram_scr, high, low_part, basis, rows_scr
    )

    (
        move_send, move_recv, pair_send, pair_recv, spread_send, spread_recv, pass_send, pass_recv,
    ) = sems[24:]
    moves = {}
    for d in range(1, blocks):
        to = lax.rem(b + d, blocks)
        moves[d] = remote(
            pred.at[to], recv.at[d], move_send.at[d], move_recv.at[d], person, to
        )
        moves[d].start()

    count = TRAITS * LAMBDAS
    mix = chebyshev_mix(count, LAMBDAS, count, factors, radius)
    ridge_ref[...] = jnp.dot(mix, basis[...], precision=HIGHEST, preferred_element_type=F32)
    pick = (
        (iota((SLOT, TRAITS), 0) == LAMBDAS) & (iota((SLOT, TRAITS), 1) == b)
    ).astype(F32).astype(BF16)
    trait_row = jnp.dot(pick, y_ref[...], preferred_element_type=F32)
    width = recv.shape[2]

    def place(block, values):
        values = values.astype(F32)
        at = pl.ds(pl.multiple_of(block * SLOT, SLOT), LAMBDAS)
        for part in range(PARTS):
            stacked[at, part * width:(part + 1) * width] = values[
                part * LAMBDAS:(part + 1) * LAMBDAS, :
            ]

    place(b, pred[b])
    for d in range(1, blocks):
        moves[d].wait_recv()
        place(lax.rem(b + blocks - d, blocks), recv[d])
    stacked[LAMBDAS:LAMBDAS + 1, :] = trait_row[LAMBDAS:LAMBDAS + 1, :]

    w = stacked[...].astype(BF16)
    gram = lax.dot_general(w, w, CONTRACT_LANES, preferred_element_type=F32)

    size = blocks * LAMBDAS
    part = size // 2
    square = (TILE, TILE)
    row, lane = iota(square, 0), iota(square, 1)
    cols_a = ((lane < size) & (row == slot_of(lane))) | ((lane == 120) & (row == LAMBDAS))
    cols_b = (
        (lane >= size) & (lane < size + part) & (row == slot_of(lane - part))
    ) | ((lane == 121) & (row == LAMBDAS))
    strip = (packed.shape[0], TILE)
    row, lane = iota(strip, 0), iota(strip, 1)
    rows_a = (row < part) & (lane == slot_of(row))
    rows_b = (row < part) & (lane == slot_of(row + part))

    def select(left, right):
        inner = jnp.dot(
            gram, right.astype(F32), precision=HIGHEST, preferred_element_type=F32
        )
        return jnp.dot(
            left.astype(F32), inner, precision=HIGHEST, preferred_element_type=F32
        )

    packed[...] = select(rows_a, cols_a) + select(rows_b, cols_b)

    rows = packed.shape[0] // 2

    def side(core):
        return pl.ds(pl.multiple_of(core * rows, 8), rows)

    pair = remote(packed.at[side(other)], last_half, pair_send, pair_recv, 2 * z + other, b)
    pair.start()
    pair.wait()
    last_mine[...] = packed[side(c), :] + last_half[...]
    spread = {}
    for d in far_first(chips):
        spread[d] = remote(
            last_mine, last_slots.at[z], spread_send.at[d], spread_recv.at[d],
            2 * lax.rem(z + d, chips) + c, b,
        )
        spread[d].start()
    last_slots[z] = last_mine[...]
    for d in near_first(chips):
        spread[d].wait_recv()
    total = last_slots[0]
    for chip in range(1, chips):
        total = total + last_slots[chip]
    final[side(c), :] = total
    passed = remote(final.at[side(c)], final.at[side(c)], pass_send, pass_recv, 2 * z + other, b)
    passed.start()
    passed.wait()
    for d in range(1, chips):
        spread[d].wait_send()
    for d in range(1, blocks):
        moves[d].wait_send()

    final_ref[...] = final[...]


def finish_kernel(size, headcount, rows_ref, flat_ref, ridge_ref, gram_ref, cross_ref):
    ridge_ref[...] = rows_ref[...]
    part = size // 2
    flat = flat_ref[...]
    turned = jnp.concatenate(
        [flat, jnp.zeros((TILE - flat.shape[0], TILE), F32)], axis=0
    ).T
    shifted = pltpu.roll(flat, TILE - part, 1)
    lane = iota((part, TILE), 1)
    lower = jnp.where(lane < part, turned[part:size, :], shifted[:part, :])
    gram_ref[0, 0:part, :] = flat[:part, :size] * (1.0 / headcount)
    gram_ref[0, part:size, :] = lower[:, :size] * (1.0 / headcount)
    lane = iota((1, TILE), 1)
    pair_row = jnp.where(lane < part, turned[120:121, :], pltpu.roll(turned[121:122, :], part, 1))
    cross_ref[...] = pair_row[:, :size] * (1.0 / math.sqrt(headcount))


VMEM = pl.BlockSpec(memory_space=pltpu.VMEM)
DMA = pltpu.SemaphoreType.DMA


def per_device(chips, blocks, x, y, factors):
    people = x.shape[0]
    headcount = float(people * chips * 2)
    peers = chips // 2
    half = VARS // 2
    width = people // PARTS
    size = blocks * LAMBDAS
    rows = 48
    rows_shape = jax.ShapeDtypeStruct((TRAITS * LAMBDAS, VARS), F32)
    ridge, final = pl.pallas_call(
        functools.partial(whole_kernel, chips, blocks, headcount),
        in_specs=[
            VMEM,
            pl.BlockSpec(memory_space=pltpu.SMEM),
            pl.BlockSpec(memory_space=pl.ANY),
        ],
        out_specs=[VMEM, VMEM],
        out_shape=[rows_shape, jax.ShapeDtypeStruct((rows, TILE), F32)],
        scratch_shapes=[
            pltpu.VMEM((people, VARS), BF16),
            pltpu.VMEM((TOTAL_ROWS, TILE), F32),
            pltpu.VMEM((half, VARS), F32),
            pltpu.VMEM((half, half), F32),
            pltpu.VMEM((2 * TRAITS, VARS), F32),
            pltpu.VMEM((TOTAL_ROWS, TILE), F32),
            *(
                pltpu.VMEM(shape, F32)
                for _, count in SETS
                for shape in (
                    (count // 2, TILE), (count // 2, TILE), (count // 4, TILE), (count // 4, TILE),
                    (peers, count // (2 * chips), TILE),
                )
            ),
            pltpu.VMEM((VARS, VARS), F32),
            pltpu.VMEM((VARS, VARS), BF16),
            pltpu.VMEM((VARS, VARS), BF16),
            pltpu.VMEM((ITERS * TRAITS, VARS), F32),
            pltpu.VMEM((TRAITS, PARTS * LAMBDAS, width), F32),
            pltpu.VMEM((TRAITS, PARTS * LAMBDAS, width), BF16),
            pltpu.VMEM((blocks, PARTS * LAMBDAS, width), BF16),
            pltpu.VMEM((blocks * SLOT, people), F32),
            pltpu.VMEM((rows, TILE), F32),
            pltpu.VMEM((rows // 2, TILE), F32),
            pltpu.VMEM((rows // 2, TILE), F32),
            pltpu.VMEM((chips, rows // 2, TILE), F32),
            pltpu.VMEM((rows, TILE), F32),
            DMA((CHUNKS,)),
            *(
                DMA(shape)
                for _ in SETS
                for shape in 4 * [()] + 6 * [(peers,)] + 2 * [(chips,)]
            ),
            DMA((blocks,)), DMA((blocks,)), DMA, DMA, DMA((chips,)), DMA((chips,)), DMA, DMA,
        ],
        compiler_params=pltpu.CompilerParams(collective_id=0, has_side_effects=True),
        name="whole",
    )(y.T, factors, x)
    ridge, gram, cross = pl.pallas_call(
        functools.partial(finish_kernel, size, headcount),
        in_specs=[VMEM, VMEM],
        out_specs=[VMEM, VMEM, VMEM],
        out_shape=[
            rows_shape,
            jax.ShapeDtypeStruct((1, size, size), F32),
            jax.ShapeDtypeStruct((1, size), F32),
        ],
        name="finish",
    )(ridge, final)
    return ridge.T, gram, cross


def solution(mesh):
    chips = mesh.shape["people"] // 2
    return jax.shard_map(
        functools.partial(per_device, chips, mesh.shape["blocks"]),
        mesh=mesh,
        in_specs=(P("people", "blocks"), P("people", None), P()),
        out_specs=(P("blocks", None), P("blocks", None, None), P("blocks", None)),
        check_vma=False,
    )
```

```python
import functools
import math

import jax
import jax.numpy as jnp
from jax import lax
from jax.experimental import pallas as pl
from jax.experimental.pallas import tpu as pltpu
from jax.sharding import PartitionSpec as P

VARS = 512
TRAITS = 16
LAMBDAS = 5
ITERS = 8
SLOT = 8
PARTS = 16
MESH = pl.DeviceIdType.MESH
F32 = jnp.float32
BF16 = jnp.bfloat16
HIGHEST = lax.Precision.HIGHEST

CHUNKS = 8
TILE = 128
EDGE = TILE // 2
STRIPS = VARS // TILE
OFF_AT = {(0, 1): 0, (0, 2): 128, (0, 3): 256, (1, 2): 384, (1, 3): 512, (2, 3): 768}
UPPER_AT = (640, 704, 896, 960)
LOWER_AT = (1024, 1088)
CROSS_AT = 1152
SUMS_AT = CROSS_AT + TRAITS * STRIPS
TRAIT_AT = SUMS_AT + STRIPS
SETS = ((0, 768), (768, 512))
TOTAL_ROWS = 1280
CONTRACT_ROWS = (((0,), (0,)), ((), ()))
CONTRACT_LANES = (((1,), (1,)), ((), ()))


def iota(shape, dim):
    return lax.broadcasted_iota(jnp.int32, shape, dim)


def far_first(n):
    return sorted(range(1, n), key=lambda d: -min(d, n - d))


def near_first(n):
    return sorted(range(1, n), key=lambda d: min(d, n - d))


def loads(x_hbm, xs, x_sems):
    tile = xs.shape[0] // CHUNKS

    def chunk(i):
        return pl.ds(pl.multiple_of(i * tile, tile), tile)

    def load(i):
        return pltpu.make_async_copy(x_hbm.at[chunk(i)], xs.at[chunk(i)], x_sems.at[i])

    return chunk, load


def first_sums(x_hbm, xs, part, top, x_sems):
    chunk, load = loads(x_hbm, xs, x_sems)
    half = VARS // 2
    top[...] = jnp.zeros_like(top)

    def step(i, carry):
        load(i).wait()
        x = xs[chunk(i), :]
        top[...] += lax.dot_general(x[:, :half], x, CONTRACT_ROWS, preferred_element_type=F32)
        return carry

    lax.fori_loop(0, CHUNKS, step, 0)
    for (i, j), at in OFF_AT.items():
        if i < STRIPS // 2:
            part[at:at + TILE, :] = top[i * TILE:(i + 1) * TILE, j * TILE:(j + 1) * TILE]
    for i in range(STRIPS // 2):
        at, corner = UPPER_AT[i], i * TILE
        part[at:at + EDGE, :] = top[corner:corner + EDGE, corner:corner + TILE]


def second_sums(y_ref, xs, part, top, low, tail):
    chunk, _ = loads(None, xs, None)
    tile = xs.shape[0] // CHUNKS
    half = VARS // 2
    low[...] = jnp.zeros_like(low)
    tail[...] = jnp.zeros_like(tail)

    def step(i, carry):
        x = xs[chunk(i), :]
        lead = jnp.concatenate([y_ref[:, chunk(i)], jnp.ones((TRAITS, tile), BF16)], axis=0)
        low[...] += lax.dot_general(
            x[:, half:], x[:, half:], CONTRACT_ROWS, preferred_element_type=F32
        )
        tail[...] += jnp.dot(lead, x, preferred_element_type=F32)
        return carry

    lax.fori_loop(0, CHUNKS, step, 0)
    left = iota((EDGE, TILE), 1) < EDGE
    at = OFF_AT[2, 3]
    part[at:at + TILE, :] = low[:TILE, TILE:]
    for i in range(2):
        at, corner = UPPER_AT[2 + i], i * TILE
        part[at:at + EDGE, :] = low[corner:corner + EDGE, corner:corner + TILE]
    for at, source in zip(LOWER_AT, (top, low)):
        part[at:at + EDGE, :] = jnp.where(
            left, pltpu.roll(source[EDGE:TILE, :TILE], EDGE, 1),
            source[TILE + EDGE:2 * TILE, TILE:2 * TILE],
        )
    for j in range(STRIPS):
        at = CROSS_AT + j * TRAITS
        part[at:at + TRAITS, :] = tail[0:TRAITS, j * TILE:(j + 1) * TILE]
    part[SUMS_AT:, :] = jnp.zeros((TOTAL_ROWS - SUMS_AT, TILE), F32)
    for j in range(STRIPS):
        part[SUMS_AT + j:SUMS_AT + j + 1, :] = tail[
            TRAITS:TRAITS + 1, j * TILE:(j + 1) * TILE
        ]
    trait = jnp.sum(y_ref[...].astype(F32), axis=1, keepdims=True)
    small = (TRAITS, TILE)
    part[TRAIT_AT:TRAIT_AT + 1, :] = jnp.sum(
        jnp.where(iota(small, 0) == iota(small, 1), jnp.broadcast_to(trait, small), 0.0),
        axis=0, keepdims=True,
    )


def position():
    person = lax.axis_index("people")
    return lax.div(person, 2), lax.rem(person, 2), lax.axis_index("blocks")


def remote(src, dst, send, recv, people, block):
    return pltpu.make_async_remote_copy(
        src_ref=src, dst_ref=dst, send_sem=send, recv_sem=recv,
        device_id=(people, block), device_id_type=MESH,
    )


def signal(people, block):
    pl.semaphore_signal(
        pltpu.get_barrier_semaphore(), inc=1, device_id=(people, block), device_id_type=MESH
    )


def people_sum(chips, base, part, full, half, mine, other_half, ours, slots, sems):
    (
        pair_send, pair_recv, near_send, near_recv, spread_send, spread_recv,
        gather_send, gather_recv, near_back_send, near_back_recv, pass_send, pass_recv,
    ) = sems
    z, c, b = position()
    other = 1 - c
    odd, place = lax.rem(z, 2), lax.div(z, 2)
    peers = chips // 2
    near = lax.rem(z + (1 - 2 * odd) * (1 - 2 * c) + chips, chips)
    piece = slots.shape[1]
    rows = chips * piece
    side = peers * piece

    def rows_at(start, count):
        return pl.ds(pl.multiple_of(start, 8), count)

    pair = remote(
        part.at[rows_at(base + other * rows, rows)], half, pair_send, pair_recv, 2 * z + other, b
    )
    pair.start()
    yield
    pair.wait()
    mine[...] = part[rows_at(base + c * rows, rows), :] + half[...]
    swap = remote(
        mine.at[rows_at((1 - odd) * side, side)], other_half,
        near_send, near_recv, 2 * near + c, b,
    )
    swap.start()
    yield
    swap.wait()
    ours[...] = mine[rows_at(odd * side, side), :] + other_half[...]
    spread = {}
    for d in far_first(peers):
        to = lax.rem(place + d, peers)
        spread[d] = remote(
            ours.at[rows_at(to * piece, piece)], slots.at[d],
            spread_send.at[d], spread_recv.at[d], 2 * (2 * to + odd) + c, b,
        )
        spread[d].start()
    yield
    total = ours[rows_at(place * piece, piece), :]
    for d in near_first(peers):
        spread[d].wait_recv()
        total = total + slots[d]

    def own(parity, at):
        return rows_at(base + c * rows + parity * side + at * piece, piece)

    full[own(odd, place), :] = total
    here = own(odd, place)
    gather = {}
    for d in far_first(peers):
        to = 2 * (2 * lax.rem(place + d, peers) + odd) + c
        gather[d] = remote(
            full.at[here], full.at[here], gather_send.at[d], gather_recv.at[d], to, b
        )
        gather[d].start()
    yield
    back, passed = {}, {}
    for d in [0] + near_first(peers):
        if d:
            gather[d].wait_recv()
        here = own(odd, lax.rem(place + peers - d, peers))
        back[d] = remote(
            full.at[here], full.at[here], near_back_send.at[d], near_back_recv.at[d],
            2 * near + c, b,
        )
        back[d].start()
        passed[d] = remote(
            full.at[here], full.at[here], pass_send.at[d], pass_recv.at[d], 2 * z + other, b
        )
        passed[d].start()
    yield
    near_place = lax.div(near, 2)
    for d in [0] + near_first(peers):
        back[d].wait_recv()
        here = own(1 - odd, lax.rem(near_place + peers - d, peers))
        passed[peers + d] = remote(
            full.at[here], full.at[here], pass_send.at[peers + d], pass_recv.at[peers + d],
            2 * z + other, b,
        )
        passed[peers + d].start()
    yield
    for copy in passed.values():
        copy.wait()
    for d in range(peers):
        back[d].wait_send()
        if d:
            spread[d].wait_send()
            gather[d].wait_send()


def chebyshev_mix(rows, per_trait, count, factors, radius):
    shape = (rows, ITERS * TRAITS)
    row = iota(shape, 0)
    lane = iota(shape, 1)
    if per_trait == 8:
        trait = lax.shift_right_logical(row, 3)
    else:
        trait = lax.shift_right_logical(row * 205, 10)
    which = row - trait * per_trait
    degree = lax.shift_right_logical(lane, 4)
    keep = (lane - degree * TRAITS == trait) & (which < LAMBDAS) & (row < count)
    lam = jnp.zeros(shape, F32) + factors[LAMBDAS - 1]
    for k in range(LAMBDAS - 1):
        lam = jnp.where(which == k, factors[k], lam)
    middle = lam + radius
    center = middle / radius
    weight = 1.0 / center
    left = jnp.ones(shape, F32)
    heading = jnp.where(degree == 0, 1.0 / middle, 0.0)
    total = heading
    for sweep in range(1, ITERS):
        left = left * weight
        weight_next = 1.0 / (2.0 * center - weight)
        heading = weight_next * weight * heading + jnp.where(
            degree == sweep, 2.0 * weight_next / radius * left, 0.0
        )
        weight = weight_next
        total = total + heading
    return jnp.where(keep, total, 0.0)


def solve(headcount, full, factors_ref, xs, pred, gram, high, low, basis, rows_scr):
    for (i, j), at in OFF_AT.items():
        tile = full[at:at + TILE, :]
        gram[i * TILE:(i + 1) * TILE, j * TILE:(j + 1) * TILE] = tile
        gram[j * TILE:(j + 1) * TILE, i * TILE:(i + 1) * TILE] = tile.T
    left = iota((EDGE, TILE), 1) < EDGE
    for i in range(STRIPS):
        upper = full[UPPER_AT[i]:UPPER_AT[i] + EDGE, :]
        at = LOWER_AT[i // 2]
        lower = full[at:at + EDGE, :]
        if i % 2 == 0:
            lower = pltpu.roll(lower, EDGE, 1)
        turned = jnp.concatenate([upper, jnp.zeros((EDGE, TILE), F32)], axis=0).T
        columns = slice(i * TILE, (i + 1) * TILE)
        gram[i * TILE:i * TILE + EDGE, columns] = upper
        gram[i * TILE + EDGE:(i + 1) * TILE, columns] = jnp.where(left, turned[EDGE:, :], lower)
    shape = (VARS, VARS)
    eye = iota(shape, 0) == iota(shape, 1)
    parts = range(VARS // TILE)
    average = jnp.concatenate(
        [full[SUMS_AT + j:SUMS_AT + j + 1, :] for j in parts], axis=1
    ) / headcount
    average_col = jnp.sum(
        jnp.where(eye, jnp.broadcast_to(average, shape), 0.0), axis=1, keepdims=True
    )
    diagonal = jnp.where(eye, gram[...], 0.0)
    square = jnp.sum(diagonal, axis=0, keepdims=True)
    square_col = jnp.sum(diagonal, axis=1, keepdims=True)
    inverse = 1.0 / jnp.sqrt(square / headcount - average * average + 1e-05)
    inverse_col = 1.0 / jnp.sqrt(square_col / headcount - average_col * average_col + 1e-05)
    standard = (gram[...] * (1.0 / headcount) - average_col * average) * (inverse_col * inverse)
    limit = jnp.max(jnp.sum(jnp.abs(standard), axis=0, keepdims=True), axis=1, keepdims=True)
    radius = limit / 2.0
    scaled = standard * (1.0 / radius)
    first = scaled.astype(BF16)
    high[...] = first
    low[...] = (scaled - first.astype(F32)).astype(BF16)

    cross = jnp.concatenate(
        [full[CROSS_AT + j * TRAITS:CROSS_AT + (j + 1) * TRAITS, :] for j in parts], axis=1
    )
    small = (TRAITS, TILE)
    trait_col = jnp.sum(
        jnp.where(
            iota(small, 0) == iota(small, 1),
            jnp.broadcast_to(full[TRAIT_AT:TRAIT_AT + 1, :], small), 0.0,
        ),
        axis=1, keepdims=True,
    )
    response = math.sqrt(headcount) * (
        cross / headcount - average * (trait_col / headcount)
    ) * inverse

    def apply(u):
        u_high = u.astype(BF16)
        u_low = (u - u_high.astype(F32)).astype(BF16)
        both = jnp.dot(
            jnp.concatenate([u_high, u_low], axis=0), high[...], preferred_element_type=F32
        )
        return both[:TRAITS] + (
            both[TRAITS:] + jnp.dot(u_high, low[...], preferred_element_type=F32)
        )

    before, now = None, response
    basis[0:TRAITS, :] = now
    for degree in range(1, ITERS):
        step = now - apply(now)
        before, now = now, step if before is None else 2.0 * step - before
        basis[degree * TRAITS:(degree + 1) * TRAITS, :] = now

    factors = [factors_ref[k] for k in range(LAMBDAS)]
    mix = chebyshev_mix(TRAITS * SLOT, SLOT, TRAITS * SLOT, factors, radius)
    solution_rows = jnp.dot(mix, basis[...], precision=HIGHEST, preferred_element_type=F32)
    coef = (solution_rows * (inverse * (1.0 / math.sqrt(VARS)))).astype(BF16)
    offset = jnp.sum(coef.astype(F32) * average, axis=1, keepdims=True)

    width = xs.shape[0] // PARTS
    for part in range(PARTS):
        predicted = lax.dot_general(
            coef, xs[part * width:(part + 1) * width, :], CONTRACT_LANES,
            preferred_element_type=F32,
        ) - offset
        for t in range(TRAITS):
            rows_scr[t, part * LAMBDAS:(part + 1) * LAMBDAS, :] = predicted[
                t * SLOT:t * SLOT + LAMBDAS, :
            ]
    for t in range(TRAITS):
        pred[t] = rows_scr[t].astype(BF16)
    return factors, radius


def slot_of(compact):
    block = lax.shift_right_logical(compact * 205, 10)
    return block * SLOT + (compact - block * LAMBDAS)


def whole_kernel(
    chips, blocks, headcount, y_ref, factors_ref, x_hbm, ridge_ref, final_ref,
    xs, part, top, low, tail, full, *rest,
):
    buffers, rest = (rest[0:5], rest[5:10]), rest[10:]
    gram_scr, high, low_part, basis, rows_scr, pred, recv, stacked = rest[:8]
    packed, last_half, last_mine, last_slots, final, x_sems = rest[8:14]
    sems = rest[14:]
    _, load = loads(x_hbm, xs, x_sems)
    for i in range(CHUNKS):
        load(i).start()
    z, c, b = position()
    person = 2 * z + c
    other = 1 - c
    for d in range(1, chips):
        signal(2 * lax.rem(z + d, chips) + c, b)
    signal(2 * z + other, b)
    for d in range(1, blocks):
        signal(person, lax.rem(b + d, blocks))

    first_sums(x_hbm, xs, part, top, x_sems)
    pl.semaphore_wait(pltpu.get_barrier_semaphore(), blocks + chips - 1)
    stages = [
        people_sum(chips, base, part, full, *buffers[at], sems[12 * at:12 * at + 12])
        for at, (base, _) in enumerate(SETS)
    ]
    next(stages[0])
    second_sums(y_ref, xs, part, top, low, tail)
    stacked[...] = jnp.zeros_like(stacked)
    next(stages[1])
    for _ in range(6):
        for stage in stages:
            next(stage, None)
    factors, radius = solve(
        headcount, full, factors_ref, xs, pred, gram_scr, high, low_part, basis, rows_scr
    )

    (
        move_send, move_recv, pair_send, pair_recv, spread_send, spread_recv, pass_send, pass_recv,
    ) = sems[24:]
    moves = {}
    for d in range(1, blocks):
        to = lax.rem(b + d, blocks)
        moves[d] = remote(
            pred.at[to], recv.at[d], move_send.at[d], move_recv.at[d], person, to
        )
        moves[d].start()

    count = TRAITS * LAMBDAS
    mix = chebyshev_mix(count, LAMBDAS, count, factors, radius)
    ridge_ref[...] = jnp.dot(mix, basis[...], precision=HIGHEST, preferred_element_type=F32)
    pick = (
        (iota((SLOT, TRAITS), 0) == LAMBDAS) & (iota((SLOT, TRAITS), 1) == b)
    ).astype(F32).astype(BF16)
    trait_row = jnp.dot(pick, y_ref[...], preferred_element_type=F32)
    width = recv.shape[2]

    def place(block, values):
        values = values.astype(F32)
        at = pl.ds(pl.multiple_of(block * SLOT, SLOT), LAMBDAS)
        for part in range(PARTS):
            stacked[at, part * width:(part + 1) * width] = values[
                part * LAMBDAS:(part + 1) * LAMBDAS, :
            ]

    place(b, pred[b])
    for d in range(1, blocks):
        moves[d].wait_recv()
        place(lax.rem(b + blocks - d, blocks), recv[d])
    stacked[LAMBDAS:LAMBDAS + 1, :] = trait_row[LAMBDAS:LAMBDAS + 1, :]

    w = stacked[...].astype(BF16)
    gram = lax.dot_general(w, w, CONTRACT_LANES, preferred_element_type=F32)

    size = blocks * LAMBDAS
    side = size // 2
    group = packed.shape[0] * packed.shape[1]
    square = (TILE, TILE)
    row, lane = iota(square, 0), iota(square, 1)
    cols_a = (lane < side) & (row == slot_of(lane))
    cols_b = (lane < side) & (row == slot_of(lane + side))
    tall = (88, TILE)
    row, lane = iota(tall, 0), iota(tall, 1)
    rows_a = ((row < size) & (lane == slot_of(row))) | ((row == size + 1) & (lane == LAMBDAS))
    rows_b = ((row < side) & (lane == slot_of(row + side))) | (
        (row == size + 2) & (lane == LAMBDAS)
    )

    def select(left, right):
        inner = jnp.dot(
            gram, right.astype(F32), precision=HIGHEST, preferred_element_type=F32
        )
        return jnp.dot(
            left.astype(F32), inner, precision=HIGHEST, preferred_element_type=F32
        )

    form, second = select(rows_a, cols_a), select(rows_b, cols_b)
    diagonal = jnp.sum(
        jnp.where((row == lane) & (row < side), second, 0.0), axis=0, keepdims=True
    )
    form = jnp.where(((row < side) & (row > lane)) | (row == size + 2), second, form)
    form = jnp.where(row == size, diagonal, form)
    flat = form[0:group] + (
        pltpu.roll(form[group:2 * group], side, 1)
        + pltpu.roll(form[2 * group:3 * group], 2 * side, 1)
    )
    packed[0] = flat[:group // 2]
    packed[1] = flat[group // 2:]

    pair = remote(packed.at[other], last_half, pair_send, pair_recv, 2 * z + other, b)
    pair.start()
    pair.wait()
    last_mine[...] = packed[c] + last_half[...]
    spread = {}
    for d in far_first(chips):
        spread[d] = remote(
            last_mine, last_slots.at[z], spread_send.at[d], spread_recv.at[d],
            2 * lax.rem(z + d, chips) + c, b,
        )
        spread[d].start()
    last_slots[z] = last_mine[...]
    for d in near_first(chips):
        spread[d].wait_recv()
    total = last_slots[0]
    for chip in range(1, chips):
        total = total + last_slots[chip]
    final[c] = total
    passed = remote(final.at[c], final.at[c], pass_send, pass_recv, 2 * z + other, b)
    passed.start()
    passed.wait()
    for d in range(1, chips):
        spread[d].wait_send()
    for d in range(1, blocks):
        moves[d].wait_send()

    final_ref[...] = final[...]


def finish_kernel(size, headcount, rows_ref, flat_ref, ridge_ref, gram_ref, cross_ref, form):
    ridge_ref[...] = rows_ref[...]
    side = size // 2
    half = flat_ref.shape[1]
    for which in range(3):
        for core in range(2):
            at = (2 * which + core) * half
            values = flat_ref[core]
            form[at:at + half, :] = (
                pltpu.roll(values, TILE - which * side, 1) if which else values
            )

    def turn(values):
        padding = jnp.zeros((TILE - values.shape[0], TILE), F32)
        return jnp.concatenate([values, padding], axis=0).T

    mixed, corner = form[0:side, :], form[side:size, :]
    mixed_turned = turn(mixed)[:side, :]
    row, lane = iota((side, TILE), 0), iota((side, TILE), 1)
    first = jnp.where(row <= lane, mixed, mixed_turned)
    last = jnp.where(row > lane, mixed, mixed_turned)
    last = jnp.where(row == lane, form[size:size + 1, :], last)
    near = lane < side
    upper = jnp.where(near, first, pltpu.roll(turn(corner)[:side, :], side, 1))
    lower = jnp.where(near, corner, pltpu.roll(last, side, 1))
    gram_ref[0, 0:side, :] = upper[:, :size] * (1.0 / headcount)
    gram_ref[0, side:size, :] = lower[:, :size] * (1.0 / headcount)
    cross = jnp.where(
        iota((1, TILE), 1) < side, form[size + 1:size + 2, :],
        pltpu.roll(form[size + 2:size + 3, :], side, 1),
    )
    cross_ref[...] = cross[:, :size] * (1.0 / math.sqrt(headcount))


VMEM = pl.BlockSpec(memory_space=pltpu.VMEM)
DMA = pltpu.SemaphoreType.DMA


def per_device(chips, blocks, x, y, factors):
    people = x.shape[0]
    headcount = float(people * chips * 2)
    peers = chips // 2
    half = VARS // 2
    width = people // PARTS
    size = blocks * LAMBDAS
    half_rows = 14
    rows_shape = jax.ShapeDtypeStruct((TRAITS * LAMBDAS, VARS), F32)
    ridge, final = pl.pallas_call(
        functools.partial(whole_kernel, chips, blocks, headcount),
        in_specs=[
            VMEM,
            pl.BlockSpec(memory_space=pltpu.SMEM),
            pl.BlockSpec(memory_space=pl.ANY),
        ],
        out_specs=[VMEM, VMEM],
        out_shape=[rows_shape, jax.ShapeDtypeStruct((2, half_rows, TILE), F32)],
        scratch_shapes=[
            pltpu.VMEM((people, VARS), BF16),
            pltpu.VMEM((TOTAL_ROWS, TILE), F32),
            pltpu.VMEM((half, VARS), F32),
            pltpu.VMEM((half, half), F32),
            pltpu.VMEM((2 * TRAITS, VARS), F32),
            pltpu.VMEM((TOTAL_ROWS, TILE), F32),
            *(
                pltpu.VMEM(shape, F32)
                for _, count in SETS
                for shape in (
                    (count // 2, TILE), (count // 2, TILE), (count // 4, TILE), (count // 4, TILE),
                    (peers, count // (2 * chips), TILE),
                )
            ),
            pltpu.VMEM((VARS, VARS), F32),
            pltpu.VMEM((VARS, VARS), BF16),
            pltpu.VMEM((VARS, VARS), BF16),
            pltpu.VMEM((ITERS * TRAITS, VARS), F32),
            pltpu.VMEM((TRAITS, PARTS * LAMBDAS, width), F32),
            pltpu.VMEM((TRAITS, PARTS * LAMBDAS, width), BF16),
            pltpu.VMEM((blocks, PARTS * LAMBDAS, width), BF16),
            pltpu.VMEM((blocks * SLOT, people), F32),
            pltpu.VMEM((2, half_rows, TILE), F32),
            pltpu.VMEM((half_rows, TILE), F32),
            pltpu.VMEM((half_rows, TILE), F32),
            pltpu.VMEM((chips, half_rows, TILE), F32),
            pltpu.VMEM((2, half_rows, TILE), F32),
            DMA((CHUNKS,)),
            *(
                DMA(shape)
                for _ in SETS
                for shape in 4 * [()] + 6 * [(peers,)] + 2 * [(chips,)]
            ),
            DMA((blocks,)), DMA((blocks,)), DMA, DMA, DMA((chips,)), DMA((chips,)), DMA, DMA,
        ],
        compiler_params=pltpu.CompilerParams(collective_id=0, has_side_effects=True),
        name="whole",
    )(y.T, factors, x)
    ridge, gram, cross = pl.pallas_call(
        functools.partial(finish_kernel, size, headcount),
        in_specs=[VMEM, VMEM],
        out_specs=[VMEM, VMEM, VMEM],
        out_shape=[
            rows_shape,
            jax.ShapeDtypeStruct((1, size, size), F32),
            jax.ShapeDtypeStruct((1, size), F32),
        ],
        scratch_shapes=[pltpu.VMEM((88, TILE), F32)],
        name="finish",
    )(ridge, final)
    return ridge.T, gram, cross


def solution(mesh):
    chips = mesh.shape["people"] // 2
    return jax.shard_map(
        functools.partial(per_device, chips, mesh.shape["blocks"]),
        mesh=mesh,
        in_specs=(P("people", "blocks"), P("people", None), P()),
        out_specs=(P("blocks", None), P("blocks", None, None), P("blocks", None)),
        check_vma=False,
    )
```

```python
import functools
import math

import jax
import jax.numpy as jnp
from jax import lax
from jax.experimental import pallas as pl
from jax.experimental.pallas import tpu as pltpu
from jax.sharding import PartitionSpec as P

VARS = 512
TRAITS = 16
LAMBDAS = 5
ITERS = 8
SLOT = 8
PARTS = 16
MESH = pl.DeviceIdType.MESH
F32 = jnp.float32
BF16 = jnp.bfloat16
HIGHEST = lax.Precision.HIGHEST

CHUNKS = 8
TILE = 128
EDGE = TILE // 2
STRIPS = VARS // TILE
OFF_AT = {(0, 1): 0, (0, 2): 128, (0, 3): 256, (1, 2): 384, (1, 3): 512, (2, 3): 768}
UPPER_AT = (640, 704, 896, 960)
LOWER_AT = (1024, 1088)
CROSS_AT = 1152
SUMS_AT = CROSS_AT + TRAITS * STRIPS
TRAIT_AT = SUMS_AT + STRIPS
SETS = ((0, 768), (768, 512))
TOTAL_ROWS = 1280
CONTRACT_ROWS = (((0,), (0,)), ((), ()))
CONTRACT_LANES = (((1,), (1,)), ((), ()))


def iota(shape, dim):
    return lax.broadcasted_iota(jnp.int32, shape, dim)


def far_first(n):
    return sorted(range(1, n), key=lambda d: -min(d, n - d))


def near_first(n):
    return sorted(range(1, n), key=lambda d: min(d, n - d))


def loads(x_hbm, xs, x_sems):
    tile = xs.shape[0] // CHUNKS

    def chunk(i):
        return pl.ds(pl.multiple_of(i * tile, tile), tile)

    def load(i):
        return pltpu.make_async_copy(x_hbm.at[chunk(i)], xs.at[chunk(i)], x_sems.at[i])

    return chunk, load


def first_sums(x_hbm, xs, part, top, x_sems):
    chunk, load = loads(x_hbm, xs, x_sems)
    half = VARS // 2
    top[...] = jnp.zeros_like(top)

    def step(i, carry):
        load(i).wait()
        x = xs[chunk(i), :]
        top[...] += lax.dot_general(x[:, :half], x, CONTRACT_ROWS, preferred_element_type=F32)
        return carry

    lax.fori_loop(0, CHUNKS, step, 0)
    for (i, j), at in OFF_AT.items():
        if i < STRIPS // 2:
            part[at:at + TILE, :] = top[i * TILE:(i + 1) * TILE, j * TILE:(j + 1) * TILE]
    for i in range(STRIPS // 2):
        at, corner = UPPER_AT[i], i * TILE
        part[at:at + EDGE, :] = top[corner:corner + EDGE, corner:corner + TILE]


def second_sums(y_ref, xs, part, top, low, tail):
    chunk, _ = loads(None, xs, None)
    tile = xs.shape[0] // CHUNKS
    half = VARS // 2
    low[...] = jnp.zeros_like(low)
    tail[...] = jnp.zeros_like(tail)

    def step(i, carry):
        x = xs[chunk(i), :]
        lead = jnp.concatenate([y_ref[:, chunk(i)], jnp.ones((TRAITS, tile), BF16)], axis=0)
        low[...] += lax.dot_general(
            x[:, half:], x[:, half:], CONTRACT_ROWS, preferred_element_type=F32
        )
        tail[...] += jnp.dot(lead, x, preferred_element_type=F32)
        return carry

    lax.fori_loop(0, CHUNKS, step, 0)
    left = iota((EDGE, TILE), 1) < EDGE
    at = OFF_AT[2, 3]
    part[at:at + TILE, :] = low[:TILE, TILE:]
    for i in range(2):
        at, corner = UPPER_AT[2 + i], i * TILE
        part[at:at + EDGE, :] = low[corner:corner + EDGE, corner:corner + TILE]
    for at, source in zip(LOWER_AT, (top, low)):
        part[at:at + EDGE, :] = jnp.where(
            left, pltpu.roll(source[EDGE:TILE, :TILE], EDGE, 1),
            source[TILE + EDGE:2 * TILE, TILE:2 * TILE],
        )
    for j in range(STRIPS):
        at = CROSS_AT + j * TRAITS
        part[at:at + TRAITS, :] = tail[0:TRAITS, j * TILE:(j + 1) * TILE]
    part[SUMS_AT:, :] = jnp.zeros((TOTAL_ROWS - SUMS_AT, TILE), F32)
    for j in range(STRIPS):
        part[SUMS_AT + j:SUMS_AT + j + 1, :] = tail[
            TRAITS:TRAITS + 1, j * TILE:(j + 1) * TILE
        ]
    trait = jnp.sum(y_ref[...].astype(F32), axis=1, keepdims=True)
    small = (TRAITS, TILE)
    part[TRAIT_AT:TRAIT_AT + 1, :] = jnp.sum(
        jnp.where(iota(small, 0) == iota(small, 1), jnp.broadcast_to(trait, small), 0.0),
        axis=0, keepdims=True,
    )


def position():
    person = lax.axis_index("people")
    return lax.div(person, 2), lax.rem(person, 2), lax.axis_index("blocks")


def remote(src, dst, send, recv, people, block):
    return pltpu.make_async_remote_copy(
        src_ref=src, dst_ref=dst, send_sem=send, recv_sem=recv,
        device_id=(people, block), device_id_type=MESH,
    )


def signal(people, block):
    pl.semaphore_signal(
        pltpu.get_barrier_semaphore(), inc=1, device_id=(people, block), device_id_type=MESH
    )


def people_sum(chips, base, part, full, half, mine, other_half, ours, slots, sems):
    (
        pair_send, pair_recv, near_send, near_recv, spread_send, spread_recv,
        gather_send, gather_recv, near_back_send, near_back_recv, pass_send, pass_recv,
    ) = sems
    z, c, b = position()
    other = 1 - c
    odd, place = lax.rem(z, 2), lax.div(z, 2)
    peers = chips // 2
    near = lax.rem(z + (1 - 2 * odd) * (1 - 2 * c) + chips, chips)
    piece = slots.shape[1]
    rows = chips * piece
    side = peers * piece

    def rows_at(start, count):
        return pl.ds(pl.multiple_of(start, 8), count)

    pair = remote(
        part.at[rows_at(base + other * rows, rows)], half, pair_send, pair_recv, 2 * z + other, b
    )
    pair.start()
    yield
    pair.wait()
    mine[...] = part[rows_at(base + c * rows, rows), :] + half[...]
    swap = remote(
        mine.at[rows_at((1 - odd) * side, side)], other_half,
        near_send, near_recv, 2 * near + c, b,
    )
    swap.start()
    yield
    swap.wait()
    ours[...] = mine[rows_at(odd * side, side), :] + other_half[...]
    turn = 2 - 4 * c

    def at_place(step):
        return lax.rem(place + step + 2 * peers, peers)

    def person_at(step):
        return 2 * (2 * at_place(step) + odd) + c

    def rows_for(step):
        return rows_at(at_place(step) * piece, piece)

    spread = {}

    def send_piece(d, step, to):
        spread[d] = remote(
            ours.at[rows_for(step)], slots.at[d], spread_send.at[d], spread_recv.at[d],
            person_at(to), b,
        )
        spread[d].start()

    send_piece(4, 4, turn)
    send_piece(3, 3, 1)
    send_piece(5, -3, -1)
    send_piece(1, 1, 1)
    send_piece(7, -1, -1)
    yield
    for d, step in ((3, 2), (5, -2), (4, turn)):
        spread[d].wait_recv()
        ours[rows_for(step), :] = ours[rows_for(step), :] + slots[d]
    send_piece(2, 2, 2)
    send_piece(6, -2, -2)
    yield
    total = ours[rows_for(0), :]
    for d in (1, 7, 2, 6):
        spread[d].wait_recv()
        total = total + slots[d]

    def own(parity, at):
        return rows_at(base + c * rows + parity * side + at * piece, piece)

    full[own(odd, place), :] = total
    gather = {}

    def hand_on(d, step, to):
        rows_here = own(odd, at_place(step))
        gather[d] = remote(
            full.at[rows_here], full.at[rows_here], gather_send.at[d], gather_recv.at[d],
            person_at(to), b,
        )
        gather[d].start()

    hand_on(2, 0, 2)
    hand_on(6, 0, -2)
    hand_on(1, 0, 1)
    hand_on(7, 0, -1)
    yield
    back, passed = {}, {}

    def share(d):
        here = own(odd, at_place(-d))
        back[d] = remote(
            full.at[here], full.at[here], near_back_send.at[d], near_back_recv.at[d],
            2 * near + c, b,
        )
        back[d].start()
        passed[d] = remote(
            full.at[here], full.at[here], pass_send.at[d], pass_recv.at[d], 2 * z + other, b
        )
        passed[d].start()

    share(0)
    gather[2].wait_recv()
    hand_on(3, -2, 1)
    gather[6].wait_recv()
    hand_on(5, 2, -1)
    hand_on(4, -turn, turn)
    for d in (1, 7):
        gather[d].wait_recv()
        share(d)
    share(2)
    share(6)
    yield
    for d in (3, 5, 4):
        gather[d].wait_recv()
        share(d)
    yield
    near_place = lax.div(near, 2)
    for d in (0, 1, 7, 2, 6, 3, 5, 4):
        back[d].wait_recv()
        here = own(1 - odd, lax.rem(near_place + peers - d, peers))
        passed[peers + d] = remote(
            full.at[here], full.at[here], pass_send.at[peers + d], pass_recv.at[peers + d],
            2 * z + other, b,
        )
        passed[peers + d].start()
    yield
    for copy in passed.values():
        copy.wait()
    for d in range(peers):
        back[d].wait_send()
        if d:
            spread[d].wait_send()
            gather[d].wait_send()


def chebyshev_mix(rows, per_trait, count, factors, radius):
    shape = (rows, ITERS * TRAITS)
    row = iota(shape, 0)
    lane = iota(shape, 1)
    if per_trait == 8:
        trait = lax.shift_right_logical(row, 3)
    else:
        trait = lax.shift_right_logical(row * 205, 10)
    which = row - trait * per_trait
    degree = lax.shift_right_logical(lane, 4)
    keep = (lane - degree * TRAITS == trait) & (which < LAMBDAS) & (row < count)
    lam = jnp.zeros(shape, F32) + factors[LAMBDAS - 1]
    for k in range(LAMBDAS - 1):
        lam = jnp.where(which == k, factors[k], lam)
    middle = lam + radius
    center = middle / radius
    weight = 1.0 / center
    left = jnp.ones(shape, F32)
    heading = jnp.where(degree == 0, 1.0 / middle, 0.0)
    total = heading
    for sweep in range(1, ITERS):
        left = left * weight
        weight_next = 1.0 / (2.0 * center - weight)
        heading = weight_next * weight * heading + jnp.where(
            degree == sweep, 2.0 * weight_next / radius * left, 0.0
        )
        weight = weight_next
        total = total + heading
    return jnp.where(keep, total, 0.0)


def solve(headcount, full, factors_ref, xs, pred, gram, high, low, basis, rows_scr):
    for (i, j), at in OFF_AT.items():
        tile = full[at:at + TILE, :]
        gram[i * TILE:(i + 1) * TILE, j * TILE:(j + 1) * TILE] = tile
        gram[j * TILE:(j + 1) * TILE, i * TILE:(i + 1) * TILE] = tile.T
    left = iota((EDGE, TILE), 1) < EDGE
    for i in range(STRIPS):
        upper = full[UPPER_AT[i]:UPPER_AT[i] + EDGE, :]
        at = LOWER_AT[i // 2]
        lower = full[at:at + EDGE, :]
        if i % 2 == 0:
            lower = pltpu.roll(lower, EDGE, 1)
        turned = jnp.concatenate([upper, jnp.zeros((EDGE, TILE), F32)], axis=0).T
        columns = slice(i * TILE, (i + 1) * TILE)
        gram[i * TILE:i * TILE + EDGE, columns] = upper
        gram[i * TILE + EDGE:(i + 1) * TILE, columns] = jnp.where(left, turned[EDGE:, :], lower)
    shape = (VARS, VARS)
    eye = iota(shape, 0) == iota(shape, 1)
    parts = range(VARS // TILE)
    average = jnp.concatenate(
        [full[SUMS_AT + j:SUMS_AT + j + 1, :] for j in parts], axis=1
    ) / headcount
    average_col = jnp.sum(
        jnp.where(eye, jnp.broadcast_to(average, shape), 0.0), axis=1, keepdims=True
    )
    diagonal = jnp.where(eye, gram[...], 0.0)
    square = jnp.sum(diagonal, axis=0, keepdims=True)
    square_col = jnp.sum(diagonal, axis=1, keepdims=True)
    inverse = 1.0 / jnp.sqrt(square / headcount - average * average + 1e-05)
    inverse_col = 1.0 / jnp.sqrt(square_col / headcount - average_col * average_col + 1e-05)
    standard = (gram[...] * (1.0 / headcount) - average_col * average) * (inverse_col * inverse)
    limit = jnp.max(jnp.sum(jnp.abs(standard), axis=0, keepdims=True), axis=1, keepdims=True)
    radius = limit / 2.0
    scaled = standard * (1.0 / radius)
    first = scaled.astype(BF16)
    high[...] = first
    low[...] = (scaled - first.astype(F32)).astype(BF16)

    cross = jnp.concatenate(
        [full[CROSS_AT + j * TRAITS:CROSS_AT + (j + 1) * TRAITS, :] for j in parts], axis=1
    )
    small = (TRAITS, TILE)
    trait_col = jnp.sum(
        jnp.where(
            iota(small, 0) == iota(small, 1),
            jnp.broadcast_to(full[TRAIT_AT:TRAIT_AT + 1, :], small), 0.0,
        ),
        axis=1, keepdims=True,
    )
    response = math.sqrt(headcount) * (
        cross / headcount - average * (trait_col / headcount)
    ) * inverse

    def apply(u):
        u_high = u.astype(BF16)
        u_low = (u - u_high.astype(F32)).astype(BF16)
        both = jnp.dot(
            jnp.concatenate([u_high, u_low], axis=0), high[...], preferred_element_type=F32
        )
        return both[:TRAITS] + (
            both[TRAITS:] + jnp.dot(u_high, low[...], preferred_element_type=F32)
        )

    before, now = None, response
    basis[0:TRAITS, :] = now
    for degree in range(1, ITERS):
        step = now - apply(now)
        before, now = now, step if before is None else 2.0 * step - before
        basis[degree * TRAITS:(degree + 1) * TRAITS, :] = now

    factors = [factors_ref[k] for k in range(LAMBDAS)]
    mix = chebyshev_mix(TRAITS * SLOT, SLOT, TRAITS * SLOT, factors, radius)
    solution_rows = jnp.dot(mix, basis[...], precision=HIGHEST, preferred_element_type=F32)
    coef = (solution_rows * (inverse * (1.0 / math.sqrt(VARS)))).astype(BF16)
    offset = jnp.sum(coef.astype(F32) * average, axis=1, keepdims=True)

    width = xs.shape[0] // PARTS
    for part in range(PARTS):
        predicted = lax.dot_general(
            coef, xs[part * width:(part + 1) * width, :], CONTRACT_LANES,
            preferred_element_type=F32,
        ) - offset
        for t in range(TRAITS):
            rows_scr[t, part * LAMBDAS:(part + 1) * LAMBDAS, :] = predicted[
                t * SLOT:t * SLOT + LAMBDAS, :
            ]
    for t in range(TRAITS):
        pred[t] = rows_scr[t].astype(BF16)
    return factors, radius


def slot_of(compact):
    block = lax.shift_right_logical(compact * 205, 10)
    return block * SLOT + (compact - block * LAMBDAS)


def whole_kernel(
    chips, blocks, headcount, y_ref, factors_ref, x_hbm, ridge_ref, final_ref,
    xs, part, top, low, tail, full, *rest,
):
    buffers, rest = (rest[0:5], rest[5:10]), rest[10:]
    gram_scr, high, low_part, basis, rows_scr, pred, recv, stacked = rest[:8]
    packed, last_half, last_mine, last_slots, final, x_sems = rest[8:14]
    sems = rest[14:]
    _, load = loads(x_hbm, xs, x_sems)
    for i in range(CHUNKS):
        load(i).start()
    z, c, b = position()
    person = 2 * z + c
    other = 1 - c
    for d in range(1, chips):
        signal(2 * lax.rem(z + d, chips) + c, b)
    signal(2 * z + other, b)
    for d in range(1, blocks):
        signal(person, lax.rem(b + d, blocks))

    first_sums(x_hbm, xs, part, top, x_sems)
    pl.semaphore_wait(pltpu.get_barrier_semaphore(), blocks + chips - 1)
    stages = [
        people_sum(chips, base, part, full, *buffers[at], sems[12 * at:12 * at + 12])
        for at, (base, _) in enumerate(SETS)
    ]
    next(stages[0])
    second_sums(y_ref, xs, part, top, low, tail)
    stacked[...] = jnp.zeros_like(stacked)
    next(stages[1])
    for _ in range(8):
        for stage in stages:
            next(stage, None)
    factors, radius = solve(
        headcount, full, factors_ref, xs, pred, gram_scr, high, low_part, basis, rows_scr
    )

    (
        move_send, move_recv, pair_send, pair_recv, spread_send, spread_recv, pass_send, pass_recv,
    ) = sems[24:]
    moves = {}
    for d in range(1, blocks):
        to = lax.rem(b + d, blocks)
        moves[d] = remote(
            pred.at[to], recv.at[d], move_send.at[d], move_recv.at[d], person, to
        )
        moves[d].start()

    count = TRAITS * LAMBDAS
    mix = chebyshev_mix(count, LAMBDAS, count, factors, radius)
    ridge_ref[...] = jnp.dot(mix, basis[...], precision=HIGHEST, preferred_element_type=F32)
    pick = (
        (iota((SLOT, TRAITS), 0) == LAMBDAS) & (iota((SLOT, TRAITS), 1) == b)
    ).astype(F32).astype(BF16)
    trait_row = jnp.dot(pick, y_ref[...], preferred_element_type=F32)
    width = recv.shape[2]

    def place(block, values):
        values = values.astype(F32)
        at = pl.ds(pl.multiple_of(block * SLOT, SLOT), LAMBDAS)
        for part in range(PARTS):
            stacked[at, part * width:(part + 1) * width] = values[
                part * LAMBDAS:(part + 1) * LAMBDAS, :
            ]

    place(b, pred[b])
    for d in range(1, blocks):
        moves[d].wait_recv()
        place(lax.rem(b + blocks - d, blocks), recv[d])
    stacked[LAMBDAS:LAMBDAS + 1, :] = trait_row[LAMBDAS:LAMBDAS + 1, :]

    w = stacked[...].astype(BF16)
    gram = lax.dot_general(w, w, CONTRACT_LANES, preferred_element_type=F32)

    size = blocks * LAMBDAS
    side = size // 2
    group = packed.shape[0] * packed.shape[1]
    square = (TILE, TILE)
    row, lane = iota(square, 0), iota(square, 1)
    cols_a = (lane < side) & (row == slot_of(lane))
    cols_b = (lane < side) & (row == slot_of(lane + side))
    tall = (88, TILE)
    row, lane = iota(tall, 0), iota(tall, 1)
    rows_a = ((row < size) & (lane == slot_of(row))) | ((row == size + 1) & (lane == LAMBDAS))
    rows_b = ((row < side) & (lane == slot_of(row + side))) | (
        (row == size + 2) & (lane == LAMBDAS)
    )

    def select(left, right):
        inner = jnp.dot(
            gram, right.astype(F32), precision=HIGHEST, preferred_element_type=F32
        )
        return jnp.dot(
            left.astype(F32), inner, precision=HIGHEST, preferred_element_type=F32
        )

    form, second = select(rows_a, cols_a), select(rows_b, cols_b)
    diagonal = jnp.sum(
        jnp.where((row == lane) & (row < side), second, 0.0), axis=0, keepdims=True
    )
    form = jnp.where(((row < side) & (row > lane)) | (row == size + 2), second, form)
    form = jnp.where(row == size, diagonal, form)
    flat = form[0:group] + (
        pltpu.roll(form[group:2 * group], side, 1)
        + pltpu.roll(form[2 * group:3 * group], 2 * side, 1)
    )
    packed[0] = flat[:group // 2]
    packed[1] = flat[group // 2:]

    pair = remote(packed.at[other], last_half, pair_send, pair_recv, 2 * z + other, b)
    pair.start()
    pair.wait()
    last_mine[...] = packed[c] + last_half[...]
    spread = {}
    for d in far_first(chips):
        spread[d] = remote(
            last_mine, last_slots.at[z], spread_send.at[d], spread_recv.at[d],
            2 * lax.rem(z + d, chips) + c, b,
        )
        spread[d].start()
    last_slots[z] = last_mine[...]
    for d in near_first(chips):
        spread[d].wait_recv()
    total = last_slots[0]
    for chip in range(1, chips):
        total = total + last_slots[chip]
    final[c] = total
    passed = remote(final.at[c], final.at[c], pass_send, pass_recv, 2 * z + other, b)
    passed.start()
    passed.wait()
    for d in range(1, chips):
        spread[d].wait_send()
    for d in range(1, blocks):
        moves[d].wait_send()

    final_ref[...] = final[...]


def finish_kernel(size, headcount, rows_ref, flat_ref, ridge_ref, gram_ref, cross_ref, form):
    ridge_ref[...] = rows_ref[...]
    side = size // 2
    half = flat_ref.shape[1]
    for which in range(3):
        for core in range(2):
            at = (2 * which + core) * half
            values = flat_ref[core]
            form[at:at + half, :] = (
                pltpu.roll(values, TILE - which * side, 1) if which else values
            )

    def turn(values):
        padding = jnp.zeros((TILE - values.shape[0], TILE), F32)
        return jnp.concatenate([values, padding], axis=0).T

    mixed, corner = form[0:side, :], form[side:size, :]
    mixed_turned = turn(mixed)[:side, :]
    row, lane = iota((side, TILE), 0), iota((side, TILE), 1)
    first = jnp.where(row <= lane, mixed, mixed_turned)
    last = jnp.where(row > lane, mixed, mixed_turned)
    last = jnp.where(row == lane, form[size:size + 1, :], last)
    near = lane < side
    upper = jnp.where(near, first, pltpu.roll(turn(corner)[:side, :], side, 1))
    lower = jnp.where(near, corner, pltpu.roll(last, side, 1))
    gram_ref[0, 0:side, :] = upper[:, :size] * (1.0 / headcount)
    gram_ref[0, side:size, :] = lower[:, :size] * (1.0 / headcount)
    cross = jnp.where(
        iota((1, TILE), 1) < side, form[size + 1:size + 2, :],
        pltpu.roll(form[size + 2:size + 3, :], side, 1),
    )
    cross_ref[...] = cross[:, :size] * (1.0 / math.sqrt(headcount))


VMEM = pl.BlockSpec(memory_space=pltpu.VMEM)
DMA = pltpu.SemaphoreType.DMA


def per_device(chips, blocks, x, y, factors):
    people = x.shape[0]
    headcount = float(people * chips * 2)
    peers = chips // 2
    half = VARS // 2
    width = people // PARTS
    size = blocks * LAMBDAS
    half_rows = 14
    rows_shape = jax.ShapeDtypeStruct((TRAITS * LAMBDAS, VARS), F32)
    ridge, final = pl.pallas_call(
        functools.partial(whole_kernel, chips, blocks, headcount),
        in_specs=[
            VMEM,
            pl.BlockSpec(memory_space=pltpu.SMEM),
            pl.BlockSpec(memory_space=pl.ANY),
        ],
        out_specs=[VMEM, VMEM],
        out_shape=[rows_shape, jax.ShapeDtypeStruct((2, half_rows, TILE), F32)],
        scratch_shapes=[
            pltpu.VMEM((people, VARS), BF16),
            pltpu.VMEM((TOTAL_ROWS, TILE), F32),
            pltpu.VMEM((half, VARS), F32),
            pltpu.VMEM((half, half), F32),
            pltpu.VMEM((2 * TRAITS, VARS), F32),
            pltpu.VMEM((TOTAL_ROWS, TILE), F32),
            *(
                pltpu.VMEM(shape, F32)
                for _, count in SETS
                for shape in (
                    (count // 2, TILE), (count // 2, TILE), (count // 4, TILE), (count // 4, TILE),
                    (peers, count // (2 * chips), TILE),
                )
            ),
            pltpu.VMEM((VARS, VARS), F32),
            pltpu.VMEM((VARS, VARS), BF16),
            pltpu.VMEM((VARS, VARS), BF16),
            pltpu.VMEM((ITERS * TRAITS, VARS), F32),
            pltpu.VMEM((TRAITS, PARTS * LAMBDAS, width), F32),
            pltpu.VMEM((TRAITS, PARTS * LAMBDAS, width), BF16),
            pltpu.VMEM((blocks, PARTS * LAMBDAS, width), BF16),
            pltpu.VMEM((blocks * SLOT, people), F32),
            pltpu.VMEM((2, half_rows, TILE), F32),
            pltpu.VMEM((half_rows, TILE), F32),
            pltpu.VMEM((half_rows, TILE), F32),
            pltpu.VMEM((chips, half_rows, TILE), F32),
            pltpu.VMEM((2, half_rows, TILE), F32),
            DMA((CHUNKS,)),
            *(
                DMA(shape)
                for _ in SETS
                for shape in 4 * [()] + 6 * [(peers,)] + 2 * [(chips,)]
            ),
            DMA((blocks,)), DMA((blocks,)), DMA, DMA, DMA((chips,)), DMA((chips,)), DMA, DMA,
        ],
        compiler_params=pltpu.CompilerParams(collective_id=0, has_side_effects=True),
        name="whole",
    )(y.T, factors, x)
    ridge, gram, cross = pl.pallas_call(
        functools.partial(finish_kernel, size, headcount),
        in_specs=[VMEM, VMEM],
        out_specs=[VMEM, VMEM, VMEM],
        out_shape=[
            rows_shape,
            jax.ShapeDtypeStruct((1, size, size), F32),
            jax.ShapeDtypeStruct((1, size), F32),
        ],
        scratch_shapes=[pltpu.VMEM((88, TILE), F32)],
        name="finish",
    )(ridge, final)
    return ridge.T, gram, cross


def solution(mesh):
    chips = mesh.shape["people"] // 2
    return jax.shard_map(
        functools.partial(per_device, chips, mesh.shape["blocks"]),
        mesh=mesh,
        in_specs=(P("people", "blocks"), P("people", None), P()),
        out_specs=(P("blocks", None), P("blocks", None, None), P("blocks", None)),
        check_vma=False,
    )
```

```python
import functools
import math

import jax
import jax.numpy as jnp
from jax import lax
from jax.experimental import pallas as pl
from jax.experimental.pallas import tpu as pltpu
from jax.sharding import PartitionSpec as P

VARS = 512
TRAITS = 16
LAMBDAS = 5
ITERS = 8
SLOT = 8
PARTS = 16
MESH = pl.DeviceIdType.MESH
F32 = jnp.float32
BF16 = jnp.bfloat16
HIGHEST = lax.Precision.HIGHEST

CHUNKS = 8
TILE = 128
EDGE = TILE // 2
STRIPS = VARS // TILE
OFF_AT = {(0, 1): 0, (0, 2): 128, (0, 3): 256, (1, 2): 384, (1, 3): 512, (2, 3): 768}
UPPER_AT = (640, 704, 896, 960)
LOWER_AT = (1024, 1088)
CROSS_AT = 1152
SUMS_AT = CROSS_AT + TRAITS * STRIPS
TRAIT_AT = SUMS_AT + STRIPS
SETS = ((0, 768), (768, 512))
TOTAL_ROWS = 1280
CONTRACT_ROWS = (((0,), (0,)), ((), ()))
CONTRACT_LANES = (((1,), (1,)), ((), ()))


def iota(shape, dim):
    return lax.broadcasted_iota(jnp.int32, shape, dim)


def far_first(n):
    return sorted(range(1, n), key=lambda d: -min(d, n - d))


def near_first(n):
    return sorted(range(1, n), key=lambda d: min(d, n - d))


def loads(x_hbm, xs, x_sems):
    tile = xs.shape[0] // CHUNKS

    def chunk(i):
        return pl.ds(pl.multiple_of(i * tile, tile), tile)

    def load(i):
        return pltpu.make_async_copy(x_hbm.at[chunk(i)], xs.at[chunk(i)], x_sems.at[i])

    return chunk, load


def first_sums(x_hbm, xs, part, top, x_sems):
    chunk, load = loads(x_hbm, xs, x_sems)
    half = VARS // 2
    top[...] = jnp.zeros_like(top)

    def step(i, carry):
        load(i).wait()
        x = xs[chunk(i), :]
        top[...] += lax.dot_general(x[:, :half], x, CONTRACT_ROWS, preferred_element_type=F32)
        return carry

    lax.fori_loop(0, CHUNKS, step, 0)
    for (i, j), at in OFF_AT.items():
        if i < STRIPS // 2:
            part[at:at + TILE, :] = top[i * TILE:(i + 1) * TILE, j * TILE:(j + 1) * TILE]
    for i in range(STRIPS // 2):
        at, corner = UPPER_AT[i], i * TILE
        part[at:at + EDGE, :] = top[corner:corner + EDGE, corner:corner + TILE]


def second_sums(y_ref, xs, part, top, low, tail):
    chunk, _ = loads(None, xs, None)
    tile = xs.shape[0] // CHUNKS
    half = VARS // 2
    low[...] = jnp.zeros_like(low)
    tail[...] = jnp.zeros_like(tail)

    def step(i, carry):
        x = xs[chunk(i), :]
        lead = jnp.concatenate([y_ref[:, chunk(i)], jnp.ones((TRAITS, tile), BF16)], axis=0)
        low[...] += lax.dot_general(
            x[:, half:], x[:, half:], CONTRACT_ROWS, preferred_element_type=F32
        )
        tail[...] += jnp.dot(lead, x, preferred_element_type=F32)
        return carry

    lax.fori_loop(0, CHUNKS, step, 0)
    left = iota((EDGE, TILE), 1) < EDGE
    at = OFF_AT[2, 3]
    part[at:at + TILE, :] = low[:TILE, TILE:]
    for i in range(2):
        at, corner = UPPER_AT[2 + i], i * TILE
        part[at:at + EDGE, :] = low[corner:corner + EDGE, corner:corner + TILE]
    for at, source in zip(LOWER_AT, (top, low)):
        part[at:at + EDGE, :] = jnp.where(
            left, pltpu.roll(source[EDGE:TILE, :TILE], EDGE, 1),
            source[TILE + EDGE:2 * TILE, TILE:2 * TILE],
        )
    for j in range(STRIPS):
        at = CROSS_AT + j * TRAITS
        part[at:at + TRAITS, :] = tail[0:TRAITS, j * TILE:(j + 1) * TILE]
    part[SUMS_AT:, :] = jnp.zeros((TOTAL_ROWS - SUMS_AT, TILE), F32)
    for j in range(STRIPS):
        part[SUMS_AT + j:SUMS_AT + j + 1, :] = tail[
            TRAITS:TRAITS + 1, j * TILE:(j + 1) * TILE
        ]
    trait = jnp.sum(y_ref[...].astype(F32), axis=1, keepdims=True)
    small = (TRAITS, TILE)
    part[TRAIT_AT:TRAIT_AT + 1, :] = jnp.sum(
        jnp.where(iota(small, 0) == iota(small, 1), jnp.broadcast_to(trait, small), 0.0),
        axis=0, keepdims=True,
    )


def position():
    person = lax.axis_index("people")
    return lax.div(person, 2), lax.rem(person, 2), lax.axis_index("blocks")


def remote(src, dst, send, recv, people, block):
    return pltpu.make_async_remote_copy(
        src_ref=src, dst_ref=dst, send_sem=send, recv_sem=recv,
        device_id=(people, block), device_id_type=MESH,
    )


def signal(people, block):
    pl.semaphore_signal(
        pltpu.get_barrier_semaphore(), inc=1, device_id=(people, block), device_id_type=MESH
    )


def people_sum(chips, base, part, full, half, mine, other_half, ours, slots, sems):
    (
        pair_send, pair_recv, near_send, near_recv, spread_send, spread_recv,
        gather_send, gather_recv, near_back_send, near_back_recv, pass_send, pass_recv,
    ) = sems
    z, c, b = position()
    other = 1 - c
    odd, place = lax.rem(z, 2), lax.div(z, 2)
    peers = chips // 2
    near = lax.rem(z + (1 - 2 * odd) * (1 - 2 * c) + chips, chips)
    piece = slots.shape[1]
    rows = chips * piece
    side = peers * piece

    def rows_at(start, count):
        return pl.ds(pl.multiple_of(start, 8), count)

    pair = remote(
        part.at[rows_at(base + other * rows, rows)], half, pair_send, pair_recv, 2 * z + other, b
    )
    pair.start()
    yield
    pair.wait()
    mine[...] = part[rows_at(base + c * rows, rows), :] + half[...]
    swap = remote(
        mine.at[rows_at((1 - odd) * side, side)], other_half,
        near_send, near_recv, 2 * near + c, b,
    )
    swap.start()
    yield
    swap.wait()
    ours[...] = mine[rows_at(odd * side, side), :] + other_half[...]
    spread = {}
    for d in far_first(peers):
        to = lax.rem(place + d, peers)
        spread[d] = remote(
            ours.at[rows_at(to * piece, piece)], slots.at[d],
            spread_send.at[d], spread_recv.at[d], 2 * (2 * to + odd) + c, b,
        )
        spread[d].start()
    yield
    total = ours[rows_at(place * piece, piece), :]
    for d in near_first(peers):
        spread[d].wait_recv()
        total = total + slots[d]

    def own(parity, at):
        return rows_at(base + c * rows + parity * side + at * piece, piece)

    full[own(odd, place), :] = total
    here = own(odd, place)
    gather = {}
    for d in far_first(peers):
        to = 2 * (2 * lax.rem(place + d, peers) + odd) + c
        gather[d] = remote(
            full.at[here], full.at[here], gather_send.at[d], gather_recv.at[d], to, b
        )
        gather[d].start()
    yield
    back, passed = {}, {}
    for d in [0] + near_first(peers):
        if d:
            gather[d].wait_recv()
        here = own(odd, lax.rem(place + peers - d, peers))
        back[d] = remote(
            full.at[here], full.at[here], near_back_send.at[d], near_back_recv.at[d],
            2 * near + c, b,
        )
        back[d].start()
        passed[d] = remote(
            full.at[here], full.at[here], pass_send.at[d], pass_recv.at[d], 2 * z + other, b
        )
        passed[d].start()
    yield
    near_place = lax.div(near, 2)
    for d in [0] + near_first(peers):
        back[d].wait_recv()
        here = own(1 - odd, lax.rem(near_place + peers - d, peers))
        passed[peers + d] = remote(
            full.at[here], full.at[here], pass_send.at[peers + d], pass_recv.at[peers + d],
            2 * z + other, b,
        )
        passed[peers + d].start()
    yield
    for copy in passed.values():
        copy.wait()
    for d in range(peers):
        back[d].wait_send()
        if d:
            spread[d].wait_send()
            gather[d].wait_send()


def chebyshev_mix(rows, per_trait, count, factors, radius):
    shape = (rows, ITERS * TRAITS)
    row = iota(shape, 0)
    lane = iota(shape, 1)
    if per_trait == 8:
        trait = lax.shift_right_logical(row, 3)
    else:
        trait = lax.shift_right_logical(row * 205, 10)
    which = row - trait * per_trait
    degree = lax.shift_right_logical(lane, 4)
    keep = (lane - degree * TRAITS == trait) & (which < LAMBDAS) & (row < count)
    lam = jnp.zeros(shape, F32) + factors[LAMBDAS - 1]
    for k in range(LAMBDAS - 1):
        lam = jnp.where(which == k, factors[k], lam)
    middle = lam + radius
    center = middle / radius
    weight = 1.0 / center
    left = jnp.ones(shape, F32)
    heading = jnp.where(degree == 0, 1.0 / middle, 0.0)
    total = heading
    for sweep in range(1, ITERS):
        left = left * weight
        weight_next = 1.0 / (2.0 * center - weight)
        heading = weight_next * weight * heading + jnp.where(
            degree == sweep, 2.0 * weight_next / radius * left, 0.0
        )
        weight = weight_next
        total = total + heading
    return jnp.where(keep, total, 0.0)


def solve(headcount, full, factors_ref, xs, pred, gram, high, low, basis, rows_scr):
    for (i, j), at in OFF_AT.items():
        tile = full[at:at + TILE, :]
        gram[i * TILE:(i + 1) * TILE, j * TILE:(j + 1) * TILE] = tile
        gram[j * TILE:(j + 1) * TILE, i * TILE:(i + 1) * TILE] = tile.T
    left = iota((EDGE, TILE), 1) < EDGE
    for i in range(STRIPS):
        upper = full[UPPER_AT[i]:UPPER_AT[i] + EDGE, :]
        at = LOWER_AT[i // 2]
        lower = full[at:at + EDGE, :]
        if i % 2 == 0:
            lower = pltpu.roll(lower, EDGE, 1)
        turned = jnp.concatenate([upper, jnp.zeros((EDGE, TILE), F32)], axis=0).T
        columns = slice(i * TILE, (i + 1) * TILE)
        gram[i * TILE:i * TILE + EDGE, columns] = upper
        gram[i * TILE + EDGE:(i + 1) * TILE, columns] = jnp.where(left, turned[EDGE:, :], lower)
    shape = (VARS, VARS)
    eye = iota(shape, 0) == iota(shape, 1)
    parts = range(VARS // TILE)
    average = jnp.concatenate(
        [full[SUMS_AT + j:SUMS_AT + j + 1, :] for j in parts], axis=1
    ) / headcount
    average_col = jnp.sum(
        jnp.where(eye, jnp.broadcast_to(average, shape), 0.0), axis=1, keepdims=True
    )
    diagonal = jnp.where(eye, gram[...], 0.0)
    square = jnp.sum(diagonal, axis=0, keepdims=True)
    square_col = jnp.sum(diagonal, axis=1, keepdims=True)
    inverse = 1.0 / jnp.sqrt(square / headcount - average * average + 1e-05)
    inverse_col = 1.0 / jnp.sqrt(square_col / headcount - average_col * average_col + 1e-05)
    standard = (gram[...] * (1.0 / headcount) - average_col * average) * (inverse_col * inverse)
    limit = jnp.max(jnp.sum(jnp.abs(standard), axis=0, keepdims=True), axis=1, keepdims=True)
    radius = limit / 2.0
    scaled = standard * (1.0 / radius)
    first = scaled.astype(BF16)
    high[...] = first
    low[...] = (scaled - first.astype(F32)).astype(BF16)

    cross = jnp.concatenate(
        [full[CROSS_AT + j * TRAITS:CROSS_AT + (j + 1) * TRAITS, :] for j in parts], axis=1
    )
    small = (TRAITS, TILE)
    trait_col = jnp.sum(
        jnp.where(
            iota(small, 0) == iota(small, 1),
            jnp.broadcast_to(full[TRAIT_AT:TRAIT_AT + 1, :], small), 0.0,
        ),
        axis=1, keepdims=True,
    )
    response = math.sqrt(headcount) * (
        cross / headcount - average * (trait_col / headcount)
    ) * inverse

    def apply(u):
        u_high = u.astype(BF16)
        u_low = (u - u_high.astype(F32)).astype(BF16)
        both = jnp.dot(
            jnp.concatenate([u_high, u_low], axis=0), high[...], preferred_element_type=F32
        )
        return both[:TRAITS] + (
            both[TRAITS:] + jnp.dot(u_high, low[...], preferred_element_type=F32)
        )

    before, now = None, response
    basis[0:TRAITS, :] = now
    for degree in range(1, ITERS):
        step = now - apply(now)
        before, now = now, step if before is None else 2.0 * step - before
        basis[degree * TRAITS:(degree + 1) * TRAITS, :] = now

    factors = [factors_ref[k] for k in range(LAMBDAS)]
    mix = chebyshev_mix(TRAITS * SLOT, SLOT, TRAITS * SLOT, factors, radius)
    solution_rows = jnp.dot(mix, basis[...], precision=HIGHEST, preferred_element_type=F32)
    coef = (solution_rows * (inverse * (1.0 / math.sqrt(VARS)))).astype(BF16)
    offset = jnp.sum(coef.astype(F32) * average, axis=1, keepdims=True)

    width = xs.shape[0] // PARTS
    for part in range(PARTS):
        predicted = lax.dot_general(
            coef, xs[part * width:(part + 1) * width, :], CONTRACT_LANES,
            preferred_element_type=F32,
        ) - offset
        for t in range(TRAITS):
            rows_scr[t, part * LAMBDAS:(part + 1) * LAMBDAS, :] = predicted[
                t * SLOT:t * SLOT + LAMBDAS, :
            ]
    for t in range(TRAITS):
        pred[t] = rows_scr[t].astype(BF16)
    return factors, radius


def grid_hops(d, blocks):
    edge = math.isqrt(blocks)
    return sum(min(step, edge - step) for step in divmod(d, edge))


def grid_shift(b, d, sign, blocks):
    edge = math.isqrt(blocks)
    dx, dy = divmod(d, edge)
    x = lax.rem(lax.div(b, edge) + edge + sign * dx, edge)
    y = lax.rem(lax.rem(b, edge) + edge + sign * dy, edge)
    return x * edge + y


def slot_of(compact):
    block = lax.shift_right_logical(compact * 205, 10)
    return block * SLOT + (compact - block * LAMBDAS)


def whole_kernel(
    chips, blocks, headcount, y_hbm, factors_hbm, x_hbm, ridge_ref, final_ref,
    xs, part, top, low, tail, full, *rest,
):
    buffers, rest = (rest[0:5], rest[5:10]), rest[10:]
    gram_scr, high, low_part, basis, rows_scr, pred, recv, stacked = rest[:8]
    packed, last_half, last_mine, last_slots, final, x_sems = rest[8:14]
    y_ref, factors_ref, y_sem, factors_sem = rest[14:18]
    sems = rest[18:]
    _, load = loads(x_hbm, xs, x_sems)
    for i in range(CHUNKS):
        load(i).start()
    y_load = pltpu.make_async_copy(y_hbm, y_ref, y_sem)
    y_load.start()
    factors_load = pltpu.make_async_copy(factors_hbm, factors_ref, factors_sem)
    factors_load.start()
    z, c, b = position()
    person = 2 * z + c
    other = 1 - c
    for d in range(1, chips):
        signal(2 * lax.rem(z + d, chips) + c, b)
    signal(2 * z + other, b)
    for d in range(1, blocks):
        signal(person, lax.rem(b + d, blocks))

    first_sums(x_hbm, xs, part, top, x_sems)
    pl.semaphore_wait(pltpu.get_barrier_semaphore(), blocks + chips - 1)
    stages = [
        people_sum(chips, base, part, full, *buffers[at], sems[12 * at:12 * at + 12])
        for at, (base, _) in enumerate(SETS)
    ]
    next(stages[0])
    y_load.wait()
    factors_load.wait()
    second_sums(y_ref, xs, part, top, low, tail)
    stacked[...] = jnp.zeros_like(stacked)
    next(stages[1])
    for _ in range(6):
        for stage in stages:
            next(stage, None)
    factors, radius = solve(
        headcount, full, factors_ref, xs, pred, gram_scr, high, low_part, basis, rows_scr
    )

    (
        move_send, move_recv, pair_send, pair_recv, spread_send, spread_recv, pass_send, pass_recv,
    ) = sems[24:]
    moves = {}
    steps = sorted(range(1, blocks), key=lambda d: grid_hops(d, blocks))
    for d in reversed(steps):
        to = grid_shift(b, d, 1, blocks)
        moves[d] = remote(
            pred.at[to], recv.at[d], move_send.at[d], move_recv.at[d], person, to
        )
        moves[d].start()

    count = TRAITS * LAMBDAS
    mix = chebyshev_mix(count, LAMBDAS, count, factors, radius)
    ridge_ref[...] = jnp.dot(mix, basis[...], precision=HIGHEST, preferred_element_type=F32)
    pick = (
        (iota((SLOT, TRAITS), 0) == LAMBDAS) & (iota((SLOT, TRAITS), 1) == b)
    ).astype(F32).astype(BF16)
    trait_row = jnp.dot(pick, y_ref[...], preferred_element_type=F32)
    width = recv.shape[2]

    def place(block, values):
        values = values.astype(F32)
        at = pl.ds(pl.multiple_of(block * SLOT, SLOT), LAMBDAS)
        for part in range(PARTS):
            stacked[at, part * width:(part + 1) * width] = values[
                part * LAMBDAS:(part + 1) * LAMBDAS, :
            ]

    place(b, pred[b])
    for d in steps:
        moves[d].wait_recv()
        place(grid_shift(b, d, -1, blocks), recv[d])
    stacked[LAMBDAS:LAMBDAS + 1, :] = trait_row[LAMBDAS:LAMBDAS + 1, :]

    w = stacked[...].astype(BF16)
    gram = lax.dot_general(w, w, CONTRACT_LANES, preferred_element_type=F32)

    size = blocks * LAMBDAS
    side = size // 2
    group = packed.shape[0] * packed.shape[1]
    square = (TILE, TILE)
    row, lane = iota(square, 0), iota(square, 1)
    cols_a = (lane < side) & (row == slot_of(lane))
    cols_b = (lane < side) & (row == slot_of(lane + side))
    tall = (88, TILE)
    row, lane = iota(tall, 0), iota(tall, 1)
    rows_a = ((row < size) & (lane == slot_of(row))) | ((row == size + 1) & (lane == LAMBDAS))
    rows_b = ((row < side) & (lane == slot_of(row + side))) | (
        (row == size + 2) & (lane == LAMBDAS)
    )

    def select(left, right):
        inner = jnp.dot(
            gram, right.astype(F32), precision=HIGHEST, preferred_element_type=F32
        )
        return jnp.dot(
            left.astype(F32), inner, precision=HIGHEST, preferred_element_type=F32
        )

    form, second = select(rows_a, cols_a), select(rows_b, cols_b)
    diagonal = jnp.sum(
        jnp.where((row == lane) & (row < side), second, 0.0), axis=0, keepdims=True
    )
    form = jnp.where(((row < side) & (row > lane)) | (row == size + 2), second, form)
    form = jnp.where(row == size, diagonal, form)
    flat = form[0:group] + (
        pltpu.roll(form[group:2 * group], side, 1)
        + pltpu.roll(form[2 * group:3 * group], 2 * side, 1)
    )
    packed[0] = flat[:group // 2]
    packed[1] = flat[group // 2:]

    pair = remote(packed.at[other], last_half, pair_send, pair_recv, 2 * z + other, b)
    pair.start()
    pair.wait()
    last_mine[...] = packed[c] + last_half[...]
    spread = {}
    for d in far_first(chips):
        spread[d] = remote(
            last_mine, last_slots.at[z], spread_send.at[d], spread_recv.at[d],
            2 * lax.rem(z + d, chips) + c, b,
        )
        spread[d].start()
    last_slots[z] = last_mine[...]
    for d in near_first(chips):
        spread[d].wait_recv()
    total = last_slots[0]
    for chip in range(1, chips):
        total = total + last_slots[chip]
    final[c] = total
    passed = remote(final.at[c], final.at[c], pass_send, pass_recv, 2 * z + other, b)
    passed.start()
    passed.wait()
    for d in range(1, chips):
        spread[d].wait_send()
    for d in range(1, blocks):
        moves[d].wait_send()

    final_ref[...] = final[...]


def finish_kernel(size, headcount, rows_ref, flat_ref, ridge_ref, gram_ref, cross_ref, form):
    ridge_ref[...] = rows_ref[...]
    side = size // 2
    half = flat_ref.shape[1]
    for which in range(3):
        for core in range(2):
            at = (2 * which + core) * half
            values = flat_ref[core]
            form[at:at + half, :] = (
                pltpu.roll(values, TILE - which * side, 1) if which else values
            )

    def turn(values):
        padding = jnp.zeros((TILE - values.shape[0], TILE), F32)
        return jnp.concatenate([values, padding], axis=0).T

    mixed, corner = form[0:side, :], form[side:size, :]
    mixed_turned = turn(mixed)[:side, :]
    row, lane = iota((side, TILE), 0), iota((side, TILE), 1)
    first = jnp.where(row <= lane, mixed, mixed_turned)
    last = jnp.where(row > lane, mixed, mixed_turned)
    last = jnp.where(row == lane, form[size:size + 1, :], last)
    near = lane < side
    upper = jnp.where(near, first, pltpu.roll(turn(corner)[:side, :], side, 1))
    lower = jnp.where(near, corner, pltpu.roll(last, side, 1))
    gram_ref[0, 0:side, :] = upper[:, :size] * (1.0 / headcount)
    gram_ref[0, side:size, :] = lower[:, :size] * (1.0 / headcount)
    cross = jnp.where(
        iota((1, TILE), 1) < side, form[size + 1:size + 2, :],
        pltpu.roll(form[size + 2:size + 3, :], side, 1),
    )
    cross_ref[...] = cross[:, :size] * (1.0 / math.sqrt(headcount))


VMEM = pl.BlockSpec(memory_space=pltpu.VMEM)
DMA = pltpu.SemaphoreType.DMA


def per_device(chips, blocks, x, y, factors):
    people = x.shape[0]
    headcount = float(people * chips * 2)
    peers = chips // 2
    half = VARS // 2
    width = people // PARTS
    size = blocks * LAMBDAS
    half_rows = 14
    rows_shape = jax.ShapeDtypeStruct((TRAITS * LAMBDAS, VARS), F32)
    ridge, final = pl.pallas_call(
        functools.partial(whole_kernel, chips, blocks, headcount),
        in_specs=[
            pl.BlockSpec(memory_space=pl.ANY),
            pl.BlockSpec(memory_space=pl.ANY),
            pl.BlockSpec(memory_space=pl.ANY),
        ],
        out_specs=[VMEM, VMEM],
        out_shape=[rows_shape, jax.ShapeDtypeStruct((2, half_rows, TILE), F32)],
        scratch_shapes=[
            pltpu.VMEM((people, VARS), BF16),
            pltpu.VMEM((TOTAL_ROWS, TILE), F32),
            pltpu.VMEM((half, VARS), F32),
            pltpu.VMEM((half, half), F32),
            pltpu.VMEM((2 * TRAITS, VARS), F32),
            pltpu.VMEM((TOTAL_ROWS, TILE), F32),
            *(
                pltpu.VMEM(shape, F32)
                for _, count in SETS
                for shape in (
                    (count // 2, TILE), (count // 2, TILE), (count // 4, TILE), (count // 4, TILE),
                    (peers, count // (2 * chips), TILE),
                )
            ),
            pltpu.VMEM((VARS, VARS), F32),
            pltpu.VMEM((VARS, VARS), BF16),
            pltpu.VMEM((VARS, VARS), BF16),
            pltpu.VMEM((ITERS * TRAITS, VARS), F32),
            pltpu.VMEM((TRAITS, PARTS * LAMBDAS, width), F32),
            pltpu.VMEM((TRAITS, PARTS * LAMBDAS, width), BF16),
            pltpu.VMEM((blocks, PARTS * LAMBDAS, width), BF16),
            pltpu.VMEM((blocks * SLOT, people), F32),
            pltpu.VMEM((2, half_rows, TILE), F32),
            pltpu.VMEM((half_rows, TILE), F32),
            pltpu.VMEM((half_rows, TILE), F32),
            pltpu.VMEM((chips, half_rows, TILE), F32),
            pltpu.VMEM((2, half_rows, TILE), F32),
            DMA((CHUNKS,)),
            pltpu.VMEM((TRAITS, people), BF16),
            pltpu.SMEM((LAMBDAS,), F32),
            DMA, DMA,
            *(
                DMA(shape)
                for _ in SETS
                for shape in 4 * [()] + 6 * [(peers,)] + 2 * [(chips,)]
            ),
            DMA((blocks,)), DMA((blocks,)), DMA, DMA, DMA((chips,)), DMA((chips,)), DMA, DMA,
        ],
        compiler_params=pltpu.CompilerParams(collective_id=0, has_side_effects=True),
        name="whole",
    )(y.T, factors, x)
    ridge, gram, cross = pl.pallas_call(
        functools.partial(finish_kernel, size, headcount),
        in_specs=[VMEM, VMEM],
        out_specs=[VMEM, VMEM, VMEM],
        out_shape=[
            rows_shape,
            jax.ShapeDtypeStruct((1, size, size), F32),
            jax.ShapeDtypeStruct((1, size), F32),
        ],
        scratch_shapes=[pltpu.VMEM((88, TILE), F32)],
        name="finish",
    )(ridge, final)
    return ridge.T, gram, cross


def solution(mesh):
    chips = mesh.shape["people"] // 2
    return jax.shard_map(
        functools.partial(per_device, chips, mesh.shape["blocks"]),
        mesh=mesh,
        in_specs=(P("people", "blocks"), P("people", None), P()),
        out_specs=(P("blocks", None), P("blocks", None, None), P("blocks", None)),
        check_vma=False,
    )
```

```python
import functools
import math

import jax
import jax.numpy as jnp
from jax import lax
from jax.experimental import pallas as pl
from jax.experimental.pallas import tpu as pltpu
from jax.sharding import PartitionSpec as P

VARS = 512
TRAITS = 16
LAMBDAS = 5
ITERS = 8
SLOT = 8
PARTS = 16
MESH = pl.DeviceIdType.MESH
F32 = jnp.float32
BF16 = jnp.bfloat16
HIGHEST = lax.Precision.HIGHEST

CHUNKS = 8
TILE = 128
EDGE = TILE // 2
STRIPS = VARS // TILE
OFF_AT = {(0, 1): 0, (0, 2): 128, (0, 3): 256, (1, 2): 384, (1, 3): 512, (2, 3): 768}
UPPER_AT = (640, 704, 896, 960)
LOWER_AT = (1024, 1088)
CROSS_AT = 1152
SUMS_AT = CROSS_AT + TRAITS * STRIPS
TRAIT_AT = SUMS_AT + STRIPS
SETS = ((0, 768), (768, 512))
TOTAL_ROWS = 1280
CONTRACT_ROWS = (((0,), (0,)), ((), ()))
CONTRACT_LANES = (((1,), (1,)), ((), ()))


def iota(shape, dim):
    return lax.broadcasted_iota(jnp.int32, shape, dim)


def far_first(n):
    return sorted(range(1, n), key=lambda d: -min(d, n - d))


def near_first(n):
    return sorted(range(1, n), key=lambda d: min(d, n - d))


def loads(x_hbm, xs, x_sems):
    tile = xs.shape[0] // CHUNKS

    def chunk(i):
        return pl.ds(pl.multiple_of(i * tile, tile), tile)

    def load(i):
        return pltpu.make_async_copy(x_hbm.at[chunk(i)], xs.at[chunk(i)], x_sems.at[i])

    return chunk, load


def first_sums(x_hbm, xs, part, top, x_sems):
    chunk, load = loads(x_hbm, xs, x_sems)
    half = VARS // 2
    top[...] = jnp.zeros_like(top)

    def step(i, carry):
        load(i).wait()
        x = xs[chunk(i), :]
        top[...] += lax.dot_general(x[:, :half], x, CONTRACT_ROWS, preferred_element_type=F32)
        return carry

    lax.fori_loop(0, CHUNKS, step, 0)
    for (i, j), at in OFF_AT.items():
        if i < STRIPS // 2:
            part[at:at + TILE, :] = top[i * TILE:(i + 1) * TILE, j * TILE:(j + 1) * TILE]
    for i in range(STRIPS // 2):
        at, corner = UPPER_AT[i], i * TILE
        part[at:at + EDGE, :] = top[corner:corner + EDGE, corner:corner + TILE]


def second_sums(y_ref, xs, part, top, low, tail):
    chunk, _ = loads(None, xs, None)
    tile = xs.shape[0] // CHUNKS
    half = VARS // 2
    low[...] = jnp.zeros_like(low)
    tail[...] = jnp.zeros_like(tail)

    def step(i, carry):
        x = xs[chunk(i), :]
        lead = jnp.concatenate([y_ref[:, chunk(i)], jnp.ones((TRAITS, tile), BF16)], axis=0)
        low[...] += lax.dot_general(
            x[:, half:], x[:, half:], CONTRACT_ROWS, preferred_element_type=F32
        )
        tail[...] += jnp.dot(lead, x, preferred_element_type=F32)
        return carry

    lax.fori_loop(0, CHUNKS, step, 0)
    left = iota((EDGE, TILE), 1) < EDGE
    at = OFF_AT[2, 3]
    part[at:at + TILE, :] = low[:TILE, TILE:]
    for i in range(2):
        at, corner = UPPER_AT[2 + i], i * TILE
        part[at:at + EDGE, :] = low[corner:corner + EDGE, corner:corner + TILE]
    for at, source in zip(LOWER_AT, (top, low)):
        part[at:at + EDGE, :] = jnp.where(
            left, pltpu.roll(source[EDGE:TILE, :TILE], EDGE, 1),
            source[TILE + EDGE:2 * TILE, TILE:2 * TILE],
        )
    for j in range(STRIPS):
        at = CROSS_AT + j * TRAITS
        part[at:at + TRAITS, :] = tail[0:TRAITS, j * TILE:(j + 1) * TILE]
    part[SUMS_AT:, :] = jnp.zeros((TOTAL_ROWS - SUMS_AT, TILE), F32)
    for j in range(STRIPS):
        part[SUMS_AT + j:SUMS_AT + j + 1, :] = tail[
            TRAITS:TRAITS + 1, j * TILE:(j + 1) * TILE
        ]
    trait = jnp.sum(y_ref[...].astype(F32), axis=1, keepdims=True)
    small = (TRAITS, TILE)
    part[TRAIT_AT:TRAIT_AT + 1, :] = jnp.sum(
        jnp.where(iota(small, 0) == iota(small, 1), jnp.broadcast_to(trait, small), 0.0),
        axis=0, keepdims=True,
    )


def position():
    person = lax.axis_index("people")
    return lax.div(person, 2), lax.rem(person, 2), lax.axis_index("blocks")


def remote(src, dst, send, recv, people, block):
    return pltpu.make_async_remote_copy(
        src_ref=src, dst_ref=dst, send_sem=send, recv_sem=recv,
        device_id=(people, block), device_id_type=MESH,
    )


def signal(people, block):
    pl.semaphore_signal(
        pltpu.get_barrier_semaphore(), inc=1, device_id=(people, block), device_id_type=MESH
    )


def people_sum(chips, base, part, full, half, mine, other_half, ours, slots, sems):
    (
        pair_send, pair_recv, near_send, near_recv, spread_send, spread_recv,
        gather_send, gather_recv, near_back_send, near_back_recv, pass_send, pass_recv,
    ) = sems
    z, c, b = position()
    other = 1 - c
    odd, place = lax.rem(z, 2), lax.div(z, 2)
    peers = chips // 2
    near = lax.rem(z + (1 - 2 * odd) * (1 - 2 * c) + chips, chips)
    piece = slots.shape[1]
    rows = chips * piece
    side = peers * piece

    def rows_at(start, count):
        return pl.ds(pl.multiple_of(start, 8), count)

    pair = remote(
        part.at[rows_at(base + other * rows, rows)], half, pair_send, pair_recv, 2 * z + other, b
    )
    pair.start()
    yield
    pair.wait()
    mine[...] = part[rows_at(base + c * rows, rows), :] + half[...]
    swap = remote(
        mine.at[rows_at((1 - odd) * side, side)], other_half,
        near_send, near_recv, 2 * near + c, b,
    )
    swap.start()
    yield
    swap.wait()
    ours[...] = mine[rows_at(odd * side, side), :] + other_half[...]
    spread = {}
    for d in far_first(peers):
        to = lax.rem(place + d, peers)
        spread[d] = remote(
            ours.at[rows_at(to * piece, piece)], slots.at[d],
            spread_send.at[d], spread_recv.at[d], 2 * (2 * to + odd) + c, b,
        )
        spread[d].start()
    yield
    total = ours[rows_at(place * piece, piece), :]
    for d in near_first(peers):
        spread[d].wait_recv()
        total = total + slots[d]

    def own(parity, at):
        return rows_at(base + c * rows + parity * side + at * piece, piece)

    full[own(odd, place), :] = total
    here = own(odd, place)
    gather = {}
    for d in far_first(peers):
        to = 2 * (2 * lax.rem(place + d, peers) + odd) + c
        gather[d] = remote(
            full.at[here], full.at[here], gather_send.at[d], gather_recv.at[d], to, b
        )
        gather[d].start()
    back, passed = {}, {}
    for d in [0] + near_first(peers):
        if d:
            gather[d].wait_recv()
        here = own(odd, lax.rem(place + peers - d, peers))
        back[d] = remote(
            full.at[here], full.at[here], near_back_send.at[d], near_back_recv.at[d],
            2 * near + c, b,
        )
        back[d].start()
        passed[d] = remote(
            full.at[here], full.at[here], pass_send.at[d], pass_recv.at[d], 2 * z + other, b
        )
        passed[d].start()
        yield
    near_place = lax.div(near, 2)
    for d in [0] + near_first(peers):
        back[d].wait_recv()
        here = own(1 - odd, lax.rem(near_place + peers - d, peers))
        passed[peers + d] = remote(
            full.at[here], full.at[here], pass_send.at[peers + d], pass_recv.at[peers + d],
            2 * z + other, b,
        )
        passed[peers + d].start()
        yield
    for copy in passed.values():
        copy.wait()
    for d in range(peers):
        back[d].wait_send()
        if d:
            spread[d].wait_send()
            gather[d].wait_send()


def chebyshev_mix(rows, per_trait, count, factors, radius):
    shape = (rows, ITERS * TRAITS)
    row = iota(shape, 0)
    lane = iota(shape, 1)
    if per_trait == 8:
        trait = lax.shift_right_logical(row, 3)
    else:
        trait = lax.shift_right_logical(row * 205, 10)
    which = row - trait * per_trait
    degree = lax.shift_right_logical(lane, 4)
    keep = (lane - degree * TRAITS == trait) & (which < LAMBDAS) & (row < count)
    lam = jnp.zeros(shape, F32) + factors[LAMBDAS - 1]
    for k in range(LAMBDAS - 1):
        lam = jnp.where(which == k, factors[k], lam)
    middle = lam + radius
    center = middle / radius
    weight = 1.0 / center
    left = jnp.ones(shape, F32)
    heading = jnp.where(degree == 0, 1.0 / middle, 0.0)
    total = heading
    for sweep in range(1, ITERS):
        left = left * weight
        weight_next = 1.0 / (2.0 * center - weight)
        heading = weight_next * weight * heading + jnp.where(
            degree == sweep, 2.0 * weight_next / radius * left, 0.0
        )
        weight = weight_next
        total = total + heading
    return jnp.where(keep, total, 0.0)


def solve(headcount, full, factors_ref, xs, pred, gram, high, low, basis, rows_scr):
    for (i, j), at in OFF_AT.items():
        tile = full[at:at + TILE, :]
        gram[i * TILE:(i + 1) * TILE, j * TILE:(j + 1) * TILE] = tile
        gram[j * TILE:(j + 1) * TILE, i * TILE:(i + 1) * TILE] = tile.T
    left = iota((EDGE, TILE), 1) < EDGE
    for i in range(STRIPS):
        upper = full[UPPER_AT[i]:UPPER_AT[i] + EDGE, :]
        at = LOWER_AT[i // 2]
        lower = full[at:at + EDGE, :]
        if i % 2 == 0:
            lower = pltpu.roll(lower, EDGE, 1)
        turned = jnp.concatenate([upper, jnp.zeros((EDGE, TILE), F32)], axis=0).T
        columns = slice(i * TILE, (i + 1) * TILE)
        gram[i * TILE:i * TILE + EDGE, columns] = upper
        gram[i * TILE + EDGE:(i + 1) * TILE, columns] = jnp.where(left, turned[EDGE:, :], lower)
    shape = (VARS, VARS)
    eye = iota(shape, 0) == iota(shape, 1)
    parts = range(VARS // TILE)
    average = jnp.concatenate(
        [full[SUMS_AT + j:SUMS_AT + j + 1, :] for j in parts], axis=1
    ) / headcount
    average_col = jnp.sum(
        jnp.where(eye, jnp.broadcast_to(average, shape), 0.0), axis=1, keepdims=True
    )
    diagonal = jnp.where(eye, gram[...], 0.0)
    square = jnp.sum(diagonal, axis=0, keepdims=True)
    square_col = jnp.sum(diagonal, axis=1, keepdims=True)
    inverse = 1.0 / jnp.sqrt(square / headcount - average * average + 1e-05)
    inverse_col = 1.0 / jnp.sqrt(square_col / headcount - average_col * average_col + 1e-05)
    standard = (gram[...] * (1.0 / headcount) - average_col * average) * (inverse_col * inverse)
    limit = jnp.max(jnp.sum(jnp.abs(standard), axis=0, keepdims=True), axis=1, keepdims=True)
    radius = limit / 2.0
    scaled = standard * (1.0 / radius)
    first = scaled.astype(BF16)
    high[...] = first
    low[...] = (scaled - first.astype(F32)).astype(BF16)

    cross = jnp.concatenate(
        [full[CROSS_AT + j * TRAITS:CROSS_AT + (j + 1) * TRAITS, :] for j in parts], axis=1
    )
    small = (TRAITS, TILE)
    trait_col = jnp.sum(
        jnp.where(
            iota(small, 0) == iota(small, 1),
            jnp.broadcast_to(full[TRAIT_AT:TRAIT_AT + 1, :], small), 0.0,
        ),
        axis=1, keepdims=True,
    )
    response = math.sqrt(headcount) * (
        cross / headcount - average * (trait_col / headcount)
    ) * inverse

    def apply(u):
        u_high = u.astype(BF16)
        u_low = (u - u_high.astype(F32)).astype(BF16)
        both = jnp.dot(
            jnp.concatenate([u_high, u_low], axis=0), high[...], preferred_element_type=F32
        )
        return both[:TRAITS] + (
            both[TRAITS:] + jnp.dot(u_high, low[...], preferred_element_type=F32)
        )

    before, now = None, response
    basis[0:TRAITS, :] = now
    for degree in range(1, ITERS):
        step = now - apply(now)
        before, now = now, step if before is None else 2.0 * step - before
        basis[degree * TRAITS:(degree + 1) * TRAITS, :] = now

    factors = [factors_ref[k] for k in range(LAMBDAS)]
    mix = chebyshev_mix(TRAITS * SLOT, SLOT, TRAITS * SLOT, factors, radius)
    solution_rows = jnp.dot(mix, basis[...], precision=HIGHEST, preferred_element_type=F32)
    coef = (solution_rows * (inverse * (1.0 / math.sqrt(VARS)))).astype(BF16)
    offset = jnp.sum(coef.astype(F32) * average, axis=1, keepdims=True)

    width = xs.shape[0] // PARTS
    for part in range(PARTS):
        predicted = lax.dot_general(
            coef, xs[part * width:(part + 1) * width, :], CONTRACT_LANES,
            preferred_element_type=F32,
        ) - offset
        for t in range(TRAITS):
            rows_scr[t, part * LAMBDAS:(part + 1) * LAMBDAS, :] = predicted[
                t * SLOT:t * SLOT + LAMBDAS, :
            ]
    for t in range(TRAITS):
        pred[t] = rows_scr[t].astype(BF16)
    return factors, radius


def grid_hops(d, blocks):
    edge = math.isqrt(blocks)
    return sum(min(step, edge - step) for step in divmod(d, edge))


def grid_shift(b, d, sign, blocks):
    edge = math.isqrt(blocks)
    dx, dy = divmod(d, edge)
    x = lax.rem(lax.div(b, edge) + edge + sign * dx, edge)
    y = lax.rem(lax.rem(b, edge) + edge + sign * dy, edge)
    return x * edge + y


def slot_of(compact):
    block = lax.shift_right_logical(compact * 205, 10)
    return block * SLOT + (compact - block * LAMBDAS)


def whole_kernel(
    chips, blocks, headcount, y_hbm, factors_hbm, x_hbm, ridge_ref, final_ref,
    xs, part, top, low, tail, full, *rest,
):
    buffers, rest = (rest[0:5], rest[5:10]), rest[10:]
    gram_scr, high, low_part, basis, rows_scr, pred, recv, stacked = rest[:8]
    packed, last_half, last_mine, last_slots, final, x_sems = rest[8:14]
    y_ref, factors_ref, y_sem, factors_sem = rest[14:18]
    sems = rest[18:]
    _, load = loads(x_hbm, xs, x_sems)
    for i in range(CHUNKS):
        load(i).start()
    y_load = pltpu.make_async_copy(y_hbm, y_ref, y_sem)
    y_load.start()
    factors_load = pltpu.make_async_copy(factors_hbm, factors_ref, factors_sem)
    factors_load.start()
    z, c, b = position()
    person = 2 * z + c
    other = 1 - c
    for d in range(1, chips):
        signal(2 * lax.rem(z + d, chips) + c, b)
    signal(2 * z + other, b)
    for d in range(1, blocks):
        signal(person, lax.rem(b + d, blocks))

    first_sums(x_hbm, xs, part, top, x_sems)
    pl.semaphore_wait(pltpu.get_barrier_semaphore(), blocks + chips - 1)
    stages = [
        people_sum(chips, base, part, full, *buffers[at], sems[12 * at:12 * at + 12])
        for at, (base, _) in enumerate(SETS)
    ]
    next(stages[0])
    y_load.wait()
    factors_load.wait()
    second_sums(y_ref, xs, part, top, low, tail)
    stacked[...] = jnp.zeros_like(stacked)
    next(stages[1])
    for _ in range(32):
        for stage in stages:
            next(stage, None)
    factors, radius = solve(
        headcount, full, factors_ref, xs, pred, gram_scr, high, low_part, basis, rows_scr
    )

    (
        move_send, move_recv, pair_send, pair_recv, spread_send, spread_recv, pass_send, pass_recv,
    ) = sems[24:]
    moves = {}
    steps = sorted(range(1, blocks), key=lambda d: grid_hops(d, blocks))
    for d in reversed(steps):
        to = grid_shift(b, d, 1, blocks)
        moves[d] = remote(
            pred.at[to], recv.at[d], move_send.at[d], move_recv.at[d], person, to
        )
        moves[d].start()

    count = TRAITS * LAMBDAS
    mix = chebyshev_mix(count, LAMBDAS, count, factors, radius)
    ridge_ref[...] = jnp.dot(mix, basis[...], precision=HIGHEST, preferred_element_type=F32)
    pick = (
        (iota((SLOT, TRAITS), 0) == LAMBDAS) & (iota((SLOT, TRAITS), 1) == b)
    ).astype(F32).astype(BF16)
    trait_row = jnp.dot(pick, y_ref[...], preferred_element_type=F32)
    width = recv.shape[2]

    def place(block, values):
        values = values.astype(F32)
        at = pl.ds(pl.multiple_of(block * SLOT, SLOT), LAMBDAS)
        for part in range(PARTS):
            stacked[at, part * width:(part + 1) * width] = values[
                part * LAMBDAS:(part + 1) * LAMBDAS, :
            ]

    place(b, pred[b])
    for d in steps:
        moves[d].wait_recv()
        place(grid_shift(b, d, -1, blocks), recv[d])
    stacked[LAMBDAS:LAMBDAS + 1, :] = trait_row[LAMBDAS:LAMBDAS + 1, :]

    w = stacked[...].astype(BF16)
    gram = lax.dot_general(w, w, CONTRACT_LANES, preferred_element_type=F32)

    size = blocks * LAMBDAS
    side = size // 2
    group = packed.shape[0] * packed.shape[1]
    square = (TILE, TILE)
    row, lane = iota(square, 0), iota(square, 1)
    cols_a = (lane < side) & (row == slot_of(lane))
    cols_b = (lane < side) & (row == slot_of(lane + side))
    tall = (88, TILE)
    row, lane = iota(tall, 0), iota(tall, 1)
    rows_a = ((row < size) & (lane == slot_of(row))) | ((row == size + 1) & (lane == LAMBDAS))
    rows_b = ((row < side) & (lane == slot_of(row + side))) | (
        (row == size + 2) & (lane == LAMBDAS)
    )

    def select(left, right):
        inner = jnp.dot(
            gram, right.astype(F32), precision=HIGHEST, preferred_element_type=F32
        )
        return jnp.dot(
            left.astype(F32), inner, precision=HIGHEST, preferred_element_type=F32
        )

    form, second = select(rows_a, cols_a), select(rows_b, cols_b)
    diagonal = jnp.sum(
        jnp.where((row == lane) & (row < side), second, 0.0), axis=0, keepdims=True
    )
    form = jnp.where(((row < side) & (row > lane)) | (row == size + 2), second, form)
    form = jnp.where(row == size, diagonal, form)
    flat = form[0:group] + (
        pltpu.roll(form[group:2 * group], side, 1)
        + pltpu.roll(form[2 * group:3 * group], 2 * side, 1)
    )
    packed[0] = flat[:group // 2]
    packed[1] = flat[group // 2:]

    pair = remote(packed.at[other], last_half, pair_send, pair_recv, 2 * z + other, b)
    pair.start()
    pair.wait()
    last_mine[...] = packed[c] + last_half[...]
    spread = {}
    for d in far_first(chips):
        spread[d] = remote(
            last_mine, last_slots.at[z], spread_send.at[d], spread_recv.at[d],
            2 * lax.rem(z + d, chips) + c, b,
        )
        spread[d].start()
    last_slots[z] = last_mine[...]
    for d in near_first(chips):
        spread[d].wait_recv()
    total = last_slots[0]
    for chip in range(1, chips):
        total = total + last_slots[chip]
    final[c] = total
    passed = remote(final.at[c], final.at[c], pass_send, pass_recv, 2 * z + other, b)
    passed.start()
    passed.wait()
    for d in range(1, chips):
        spread[d].wait_send()
    for d in range(1, blocks):
        moves[d].wait_send()

    final_ref[...] = final[...]


def finish_kernel(size, headcount, rows_ref, flat_ref, ridge_ref, gram_ref, cross_ref, form):
    ridge_ref[...] = rows_ref[...]
    side = size // 2
    half = flat_ref.shape[1]
    for which in range(3):
        for core in range(2):
            at = (2 * which + core) * half
            values = flat_ref[core]
            form[at:at + half, :] = (
                pltpu.roll(values, TILE - which * side, 1) if which else values
            )

    def turn(values):
        padding = jnp.zeros((TILE - values.shape[0], TILE), F32)
        return jnp.concatenate([values, padding], axis=0).T

    mixed, corner = form[0:side, :], form[side:size, :]
    mixed_turned = turn(mixed)[:side, :]
    row, lane = iota((side, TILE), 0), iota((side, TILE), 1)
    first = jnp.where(row <= lane, mixed, mixed_turned)
    last = jnp.where(row > lane, mixed, mixed_turned)
    last = jnp.where(row == lane, form[size:size + 1, :], last)
    near = lane < side
    upper = jnp.where(near, first, pltpu.roll(turn(corner)[:side, :], side, 1))
    lower = jnp.where(near, corner, pltpu.roll(last, side, 1))
    gram_ref[0, 0:side, :] = upper[:, :size] * (1.0 / headcount)
    gram_ref[0, side:size, :] = lower[:, :size] * (1.0 / headcount)
    cross = jnp.where(
        iota((1, TILE), 1) < side, form[size + 1:size + 2, :],
        pltpu.roll(form[size + 2:size + 3, :], side, 1),
    )
    cross_ref[...] = cross[:, :size] * (1.0 / math.sqrt(headcount))


VMEM = pl.BlockSpec(memory_space=pltpu.VMEM)
DMA = pltpu.SemaphoreType.DMA


def per_device(chips, blocks, x, y, factors):
    people = x.shape[0]
    headcount = float(people * chips * 2)
    peers = chips // 2
    half = VARS // 2
    width = people // PARTS
    size = blocks * LAMBDAS
    half_rows = 14
    rows_shape = jax.ShapeDtypeStruct((TRAITS * LAMBDAS, VARS), F32)
    ridge, final = pl.pallas_call(
        functools.partial(whole_kernel, chips, blocks, headcount),
        in_specs=[
            pl.BlockSpec(memory_space=pl.ANY),
            pl.BlockSpec(memory_space=pl.ANY),
            pl.BlockSpec(memory_space=pl.ANY),
        ],
        out_specs=[VMEM, VMEM],
        out_shape=[rows_shape, jax.ShapeDtypeStruct((2, half_rows, TILE), F32)],
        scratch_shapes=[
            pltpu.VMEM((people, VARS), BF16),
            pltpu.VMEM((TOTAL_ROWS, TILE), F32),
            pltpu.VMEM((half, VARS), F32),
            pltpu.VMEM((half, half), F32),
            pltpu.VMEM((2 * TRAITS, VARS), F32),
            pltpu.VMEM((TOTAL_ROWS, TILE), F32),
            *(
                pltpu.VMEM(shape, F32)
                for _, count in SETS
                for shape in (
                    (count // 2, TILE), (count // 2, TILE), (count // 4, TILE), (count // 4, TILE),
                    (peers, count // (2 * chips), TILE),
                )
            ),
            pltpu.VMEM((VARS, VARS), F32),
            pltpu.VMEM((VARS, VARS), BF16),
            pltpu.VMEM((VARS, VARS), BF16),
            pltpu.VMEM((ITERS * TRAITS, VARS), F32),
            pltpu.VMEM((TRAITS, PARTS * LAMBDAS, width), F32),
            pltpu.VMEM((TRAITS, PARTS * LAMBDAS, width), BF16),
            pltpu.VMEM((blocks, PARTS * LAMBDAS, width), BF16),
            pltpu.VMEM((blocks * SLOT, people), F32),
            pltpu.VMEM((2, half_rows, TILE), F32),
            pltpu.VMEM((half_rows, TILE), F32),
            pltpu.VMEM((half_rows, TILE), F32),
            pltpu.VMEM((chips, half_rows, TILE), F32),
            pltpu.VMEM((2, half_rows, TILE), F32),
            DMA((CHUNKS,)),
            pltpu.VMEM((TRAITS, people), BF16),
            pltpu.SMEM((LAMBDAS,), F32),
            DMA, DMA,
            *(
                DMA(shape)
                for _ in SETS
                for shape in 4 * [()] + 6 * [(peers,)] + 2 * [(chips,)]
            ),
            DMA((blocks,)), DMA((blocks,)), DMA, DMA, DMA((chips,)), DMA((chips,)), DMA, DMA,
        ],
        compiler_params=pltpu.CompilerParams(collective_id=0, has_side_effects=True),
        name="whole",
    )(y.T, factors, x)
    ridge, gram, cross = pl.pallas_call(
        functools.partial(finish_kernel, size, headcount),
        in_specs=[VMEM, VMEM],
        out_specs=[VMEM, VMEM, VMEM],
        out_shape=[
            rows_shape,
            jax.ShapeDtypeStruct((1, size, size), F32),
            jax.ShapeDtypeStruct((1, size), F32),
        ],
        scratch_shapes=[pltpu.VMEM((88, TILE), F32)],
        name="finish",
    )(ridge, final)
    return ridge.T, gram, cross


def solution(mesh):
    chips = mesh.shape["people"] // 2
    return jax.shard_map(
        functools.partial(per_device, chips, mesh.shape["blocks"]),
        mesh=mesh,
        in_specs=(P("people", "blocks"), P("people", None), P()),
        out_specs=(P("blocks", None), P("blocks", None, None), P("blocks", None)),
        check_vma=False,
    )
```
